128 devices in a mesh: ping: 16 (over x, z), band: 8 (over y, core).
Axes of the slice: x: 4, y: 4, z: 4, core: 2. Of those that a mesh axis runs over, the one named last changes fastest.
Arguments:
- echoes: bfloat16 [2048, 8, 2, 8192], P(('ping', 'band')), may hold values from -6 to 6
- replica: bfloat16 [8, 2, 128], replicated, may hold values from -0.375 to 0.375
- steering: bfloat16 [2, 64, 64], replicated, may hold values from -0.5 to 0.5
- angle_weights: bfloat16 [2, 128, 64], replicated, may hold values from -0.75 to 0.75
- range_weights: bfloat16 [64, 384, 128], P('band'), may hold values from -0.3125 to 0.3125
- range_offsets: int32 [64], P('band'), may hold values from 0 to 5
- merge_owner: int32 [256], replicated, may hold values from -1 to 15, as said below
- merge_slot: int32 [256], replicated, may hold values from 0 to 7
Outputs:
- merged: bfloat16 [128, 2, 128, 8192], P('ping', None, None, 'band')
The draws below stay inside these ranges and needn't reach their ends.
Inputs may be any that keep to these rules, and one draw needn't show every extreme that they name: `merge_owner`: -1 marks a block that is not kept. Among the 16 blocks of one ping index (aligned blocks of the list) at most 2 name the same owner, and in every draw one owner is named by exactly 2 blocks of every ping index.
All inputs are finite; a program needn't handle non-finite values.
Results may differ from the reference program's by a relative error of at most 0.007.
Values may be sent and summed in bfloat16 or wider, within the bound.
No kernel may reach another device: no remote copies, remote signals or barrier semaphores. Data moves between devices by JAX's collectives and lax.ppermute only.
A program may use at most 128 MiB of HBM per device.

```python
import jax
import jax.numpy as jnp
from jax import lax

CHANNELS = 8
TAPS = 128
RANGE_BINS = 8192
SUB_PINGS = 8
BEAMS = 64
ANGLES = 128
BLOCKS_DEV = 16
ELEMENTS = 64
PINGS = 2048
NBLOCKS = 256
CAPACITY = 2
OUT_SLOTS = 8
BAND_BINS = 1024
BAND_BLOCKS = 8
N_PING = 16


def draw_merge_owner(key, part):
    hot_owner = jax.random.randint(jax.random.fold_in(key, 11), (), 0, N_PING)

    def one_source(source_key):
        others_pool = (hot_owner + 1 + jnp.arange((N_PING - 1) * CAPACITY) // CAPACITY) % N_PING
        shuffled = jax.random.permutation(jax.random.fold_in(source_key, 2), others_pool)
        remaining = shuffled[:BLOCKS_DEV - CAPACITY]
        keeping = jax.random.randint(jax.random.fold_in(source_key, 3), (BLOCKS_DEV - CAPACITY,), 0, 8) > 0
        remaining = jnp.where(keeping, remaining, -1)
        listed = jnp.concatenate([jnp.full((CAPACITY,), hot_owner, dtype=jnp.int32), remaining.astype(jnp.int32)])
        ordering = jax.random.permutation(jax.random.fold_in(source_key, 4), BLOCKS_DEV)
        return listed[ordering]
    source_keys = jax.random.split(jax.random.fold_in(key, 5), N_PING)
    return jax.vmap(one_source)(source_keys).reshape(-1).astype(jnp.int32)


def place_ends(entries, own_key, low, top_value):
    longest = entries.shape.index(max(entries.shape))
    spots = []
    for shift in (0, 1):
        where = [jax.random.randint(jax.random.fold_in(own_key, axis), (), 0, length) for axis, length in enumerate(entries.shape)]
        where[longest] = (where[longest] + shift) % entries.shape[longest]
        spots.append(tuple(where))
    return entries.at[spots[0]].set(low).at[spots[1]].set(top_value)


def block_scale(stream_key, dims, shards, smallest, top_value):
    def one(dim, shards_of):
        steps = jax.random.uniform(jax.random.fold_in(jax.random.fold_in(stream_key, 6), dim), (shards_of,), jnp.float32, smallest / len(shards), top_value / len(shards))
        return jnp.repeat(jnp.exp(steps), dims[dim] // shards_of).reshape((-1,) + (1,) * (len(dims) - dim - 1))

    loudness = one(*shards[0])
    for cut in shards[1:]:
        loudness = loudness * one(*cut)
    return loudness


def scatter_about(rng, extent, deviation, bound, shards=(), kind=jnp.bfloat16):
    values = deviation * jax.random.normal(rng, extent, jnp.float32)
    if shards:
        values = values * block_scale(rng, extent, shards, -0.22, 0.18)
    return jnp.clip(values, -bound, bound).astype(kind)


def setup_inputs(seed: int = 0) -> dict:
    streams_of = jax.random.split(jax.random.key(seed), 9)
    return {
        "echoes": scatter_about(streams_of[0], (PINGS, CHANNELS, 2, RANGE_BINS), 1.0, 6.0, ((0, 128),)),
        "replica": scatter_about(streams_of[1], (CHANNELS, 2, TAPS), (2 * TAPS) ** -0.5, 0.375),
        "steering": scatter_about(streams_of[2], (2, BEAMS, ELEMENTS), (2 * ELEMENTS) ** -0.5, 0.5),
        "angle_weights": scatter_about(streams_of[3], (2, ANGLES, BEAMS), BEAMS ** -0.5, 0.75),
        "range_weights": scatter_about(streams_of[4], (RANGE_BINS // 128, 384, 128), 384 ** -0.5, 0.3125, ((0, 8),)),
        "range_offsets": place_ends(jax.random.randint(streams_of[5], (RANGE_BINS // 128,), 0, BAND_BLOCKS - 2), jax.random.fold_in(streams_of[5], 1), 0, (BAND_BLOCKS - 2) - 1).astype(jnp.int32),
        "merge_owner": draw_merge_owner(jax.random.fold_in(streams_of[8], 71), 0),
        "merge_slot": place_ends(jax.random.randint(streams_of[7], (NBLOCKS,), 0, OUT_SLOTS), jax.random.fold_in(streams_of[7], 1), 0, OUT_SLOTS - 1).astype(jnp.int32),
    }


def toeplitz_blocks(replica):
    taps_count = replica.shape[2]
    shifts = jnp.arange(taps_count)
    row_index = jnp.arange(taps_count)[:, None]
    col_index = jnp.arange(taps_count)[None, :]
    lower_sel = ((row_index - col_index)[None] == shifts[:, None, None]).astype(jnp.float32)
    upper_sel = ((row_index - col_index + taps_count)[None] == shifts[:, None, None]).astype(jnp.float32)
    real_taps = replica[:, 0].astype(jnp.float32)
    imag_taps = replica[:, 1].astype(jnp.float32)
    high = lax.Precision.HIGHEST
    lower_real = jnp.einsum("ck,kmn->cmn", real_taps, lower_sel, precision=high)
    lower_imag = jnp.einsum("ck,kmn->cmn", imag_taps, lower_sel, precision=high)
    upper_real = jnp.einsum("ck,kmn->cmn", real_taps, upper_sel, precision=high)
    upper_imag = jnp.einsum("ck,kmn->cmn", imag_taps, upper_sel, precision=high)
    layers = [jnp.concatenate([lower_real, -lower_imag], 2), jnp.concatenate([lower_imag, lower_real], 2),
              jnp.concatenate([upper_real, -upper_imag], 2), jnp.concatenate([upper_imag, upper_real], 2)]
    return jnp.concatenate(layers, 1).astype(jnp.bfloat16)


def compress(echo_part, toeplitz):
    pings, chans, parts, bins = echo_part.shape
    taps_count = toeplitz.shape[2] // 2
    block_count = bins // taps_count
    shaped = echo_part.reshape(pings, chans, parts, block_count, taps_count)
    following = jnp.concatenate([shaped[:, :, :, 1:], jnp.zeros_like(shaped[:, :, :, :1])], axis=3)
    stacked = jnp.stack([shaped, following], axis=2)
    arranged = stacked.transpose(1, 0, 4, 2, 3, 5).reshape(chans, pings * block_count, 4 * taps_count)
    product = jnp.einsum("cix,cxy->ciy", arranged.astype(jnp.float32), toeplitz.astype(jnp.float32))
    product = product.reshape(chans, pings, block_count, 2, taps_count).transpose(1, 0, 3, 2, 4)
    return product.reshape(pings, chans, 2, bins).astype(jnp.bfloat16)


def beamform(tile, steering, sub_pings):
    pings, chans, parts, bins = tile.shape
    blocks = pings // sub_pings
    grouped = tile.reshape(blocks, sub_pings * chans, parts, bins).transpose(0, 2, 1, 3)
    grouped = grouped.reshape(blocks, 2 * sub_pings * chans, bins)
    real_steer = steering[0]
    imag_steer = steering[1]
    mixer = jnp.concatenate([jnp.concatenate([real_steer, -imag_steer], 1),
                             jnp.concatenate([imag_steer, real_steer], 1)], 0)
    beams = jnp.einsum("yx,bxr->byr", mixer.astype(jnp.float32), grouped.astype(jnp.float32))
    return beams.reshape(blocks, 2, real_steer.shape[0], bins).astype(jnp.bfloat16)


def rotate_angles(beam_image, angle_weights, parity):
    matrices = jnp.where(parity[:, None, None] == 1, angle_weights[1], angle_weights[0])
    turned = jnp.einsum("bya,bpar->bpyr", matrices.astype(jnp.float32), beam_image.astype(jnp.float32))
    return turned.astype(jnp.bfloat16)


def range_interp(turned, range_weights, starts):
    blocks, parts, angles, bins = turned.shape
    count = starts.shape[0]
    slab_rows = jax.vmap(lambda first_bin: lax.dynamic_slice_in_dim(turned, first_bin, 384, axis=3))(starts)
    flat = slab_rows.reshape(count, blocks * parts * angles, 384)
    product = jnp.einsum("qmx,qxy->qmy", flat.astype(jnp.float32), range_weights.astype(jnp.float32))
    product = product.reshape(count, blocks, parts, angles, 128).transpose(1, 2, 3, 0, 4)
    return product.reshape(blocks, parts, angles, count * 128).astype(jnp.bfloat16)


def reference(echoes, replica, steering, angle_weights, range_weights, range_offsets, merge_owner, merge_slot):
    toeplitz = toeplitz_blocks(replica)
    block_index = jnp.arange(RANGE_BINS // 128, dtype=jnp.int32)
    starts = ((block_index // BAND_BLOCKS) * BAND_BINS + range_offsets * 128).astype(jnp.int32)
    group_pings = BLOCKS_DEV * SUB_PINGS
    segments_all = jnp.where(merge_owner >= 0, merge_owner * OUT_SLOTS + merge_slot, N_PING * OUT_SLOTS).astype(jnp.int32)

    def one_group(merged, group):
        echo_part = lax.dynamic_slice_in_dim(echoes, (group * group_pings).astype(jnp.int32), group_pings, 0)
        compressed = compress(echo_part, toeplitz)
        beam_image = beamform(compressed, steering, SUB_PINGS)
        parity = (group * BLOCKS_DEV + jnp.arange(BLOCKS_DEV, dtype=jnp.int32)) % 2
        turned = rotate_angles(beam_image, angle_weights, parity)
        images = range_interp(turned, range_weights, starts)
        segment_ids = lax.dynamic_slice_in_dim(segments_all, (group * BLOCKS_DEV).astype(jnp.int32), BLOCKS_DEV, 0)
        merged = merged + jax.ops.segment_sum(images.astype(jnp.float32), segment_ids, num_segments=N_PING * OUT_SLOTS + 1)
        return merged, group

    initial = jnp.zeros((N_PING * OUT_SLOTS + 1, 2, ANGLES, RANGE_BINS), jnp.float32)
    merged, unused = lax.scan(one_group, initial, jnp.arange(N_PING, dtype=jnp.int32))
    return merged[:-1].astype(jnp.bfloat16)
```

```python
import functools

import jax
import jax.numpy as jnp
from jax import lax
from jax.experimental import pallas as pl
from jax.experimental.pallas import tpu as pltpu
from jax.sharding import PartitionSpec as P

CHUNKS = 1
VMEM_LIMIT = 56 * 1024 * 1024


def compress_kernel(x_ref, taps_ref, out_ref):
    row = lax.broadcasted_iota(jnp.int32, (128, 128), 0)
    col = lax.broadcasted_iota(jnp.int32, (128, 128), 1)
    lower, upper = [], []
    for part in range(2):
        line = jnp.broadcast_to(taps_ref[0, part : part + 1, :], (128, 128))
        circulant = pltpu.roll(line, 0, 1, stride=1, stride_axis=0)
        lower.append(jnp.where(row >= col, circulant, 0.0))
        upper.append(jnp.where(row < col, circulant, 0.0))
    weights = jnp.concatenate(
        [
            jnp.concatenate([lower[0], -lower[1]], 1),
            jnp.concatenate([lower[1], lower[0]], 1),
            jnp.concatenate([upper[0], -upper[1]], 1),
            jnp.concatenate([upper[1], upper[0]], 1),
        ],
        0,
    ).astype(jnp.bfloat16)
    wanted = (row & 7) * 16 + ((row >> 3) & 7) * 2 + (row >> 6)
    permute = (wanted == col).astype(jnp.float32).astype(jnp.bfloat16)
    for block in range(2):
        real, imag = [], []
        for tile in range(8):
            rows = x_ref[8 * block : 8 * block + 8, 0, 16 * tile : 16 * tile + 16, :]
            moved = jnp.dot(permute, rows.reshape(128, 128), preferred_element_type=jnp.float32)
            real.append(moved[:64])
            imag.append(moved[64:])
        real = jnp.concatenate(real, 0)
        imag = jnp.concatenate(imag, 0)
        nothing = jnp.zeros((8, 128), jnp.float32)
        real_next = jnp.concatenate([real[8:], nothing], 0)
        imag_next = jnp.concatenate([imag[8:], nothing], 0)
        stacked = jnp.concatenate([real, imag, real_next, imag_next], 1).astype(jnp.bfloat16)
        product = jnp.dot(stacked, weights, preferred_element_type=jnp.float32)
        product = product.reshape(64, 8, 256)
        product = jnp.concatenate([product[:, :, :128], product[:, :, 128:]], 1)
        out_ref[:, block, :, 0] = product.astype(jnp.bfloat16).reshape(8, 8, 16, 128)


def compress(x, taps, first, count):
    return pl.pallas_call(
        compress_kernel,
        grid=(count,),
        in_specs=[
            pl.BlockSpec((16, 1, 128, 128), lambda i: (0, first + i, 0, 0)),
            pl.BlockSpec((1, 2, 128), lambda i: (first + i, 0, 0)),
        ],
        out_specs=pl.BlockSpec((8, 2, 8, 1, 16, 128), lambda i: (0, 0, 0, i, 0, 0)),
        out_shape=jax.ShapeDtypeStruct((8, 2, 8, count, 16, 128), jnp.bfloat16),
        compiler_params=pltpu.CompilerParams(vmem_limit_bytes=VMEM_LIMIT),
        name="compress",
    )(x, taps)


def pack_kernel(table_ref, source_ref, out_ref, sems):
    def copy(slot):
        block = jnp.maximum(table_ref[slot], 0)
        return pltpu.make_async_copy(source_ref.at[block], out_ref.at[slot], sems.at[slot])

    for slot in range(32):
        copy(slot).start()
    for slot in range(32):
        copy(slot).wait()


def pack(table, source):
    return pl.pallas_call(
        pack_kernel,
        grid_spec=pltpu.PrefetchScalarGridSpec(
            num_scalar_prefetch=1,
            grid=(1,),
            in_specs=[pl.BlockSpec(memory_space=pl.ANY)],
            out_specs=pl.BlockSpec(memory_space=pl.ANY),
            scratch_shapes=[pltpu.SemaphoreType.DMA((32,))],
        ),
        out_shape=jax.ShapeDtypeStruct((32,) + source.shape[1:], source.dtype),
        name="pack",
    )(table, source)


def image_kernel(chunks, ids_ref, offsets_ref, *refs):
    arrived = refs[:chunks]
    angle_ref, range_ref, out_ref, total, turned = refs[chunks:]
    step = pl.program_id(0)
    height = 128 // chunks

    @pl.when(step < 8)
    def _():
        total[...] = jnp.zeros_like(total)

        def add(slot, carry):
            target = ids_ref[slot]

            @pl.when(target >= 0)
            def _():
                for chunk in range(chunks):
                    rows = pl.ds(chunk * height, height)
                    total[target, rows, :] += arrived[chunk][slot, 0].astype(jnp.float32)

            return carry

        lax.fori_loop(0, 32, add, 0)
        angle = angle_ref[...]
        for image in range(8):
            both = total[2 * image : 2 * image + 2].reshape(256, 128).astype(jnp.bfloat16)
            product = jnp.dot(angle, both, preferred_element_type=jnp.float32)
            turned[step, 256 * image : 256 * image + 256, :] = product.astype(jnp.bfloat16)

    @pl.when(step >= 8)
    def _():
        start = offsets_ref[jnp.maximum(step - 8, 0)]
        for half in range(2):
            rows = pl.ds(1024 * half, 1024)
            slab = jnp.concatenate([turned[start + i, rows, :] for i in range(3)], 1)
            product = jnp.dot(slab, range_ref[0], preferred_element_type=jnp.float32)
            out_ref[rows, :] = product.astype(jnp.bfloat16)


def form_images(ids, offsets, arrived, angle, range_weights):
    chunks = len(arrived)
    height = 128 // chunks
    return pl.pallas_call(
        functools.partial(image_kernel, chunks),
        grid_spec=pltpu.PrefetchScalarGridSpec(
            num_scalar_prefetch=2,
            grid=(16,),
            in_specs=[pl.BlockSpec((32, 1, height, 128), lambda s, *_: (0, jnp.minimum(s, 7), 0, 0))]
            * chunks
            + [
                pl.BlockSpec((256, 256), lambda s, *_: (0, 0)),
                pl.BlockSpec((1, 384, 128), lambda s, *_: (jnp.maximum(s - 8, 0), 0, 0)),
            ],
            out_specs=pl.BlockSpec((2048, 128), lambda s, *_: (0, jnp.maximum(s - 8, 0))),
            scratch_shapes=[
                pltpu.VMEM((16, 128, 128), jnp.float32),
                pltpu.VMEM((8, 2048, 128), jnp.bfloat16),
            ],
        ),
        out_shape=jax.ShapeDtypeStruct((2048, 1024), jnp.bfloat16),
        compiler_params=pltpu.CompilerParams(vmem_limit_bytes=VMEM_LIMIT),
        name="form_images",
    )(ids, offsets, *arrived, angle, range_weights)


def angle_matrix(steering, angle_weights):
    both = jnp.einsum("pya,sae->pyse", angle_weights, steering, preferred_element_type=jnp.float32)
    real, imag = both[:, :, 0], both[:, :, 1]
    full = jnp.stack([jnp.stack([real, -imag], 2), jnp.stack([imag, real], 2)], 0)
    full = full.astype(jnp.bfloat16).reshape(2, 2, 128, 2, 8, 8)
    return full.transpose(0, 2, 1, 5, 3, 4).reshape(256, 256)


def routing(merge_owner, merge_slot, ping_index):
    owners = merge_owner.reshape(16, 16)
    slots = merge_slot.reshape(16, 16)
    place = jnp.arange(16, dtype=jnp.int32)
    same = (owners[:, :, None] == owners[:, None, :]) & (place[None, :, None] > place[None, None, :])
    rank = jnp.sum(same.astype(jnp.int32), 2)
    pair = jnp.arange(2, dtype=jnp.int32)
    mine = lax.dynamic_index_in_dim(owners, ping_index, 0, keepdims=False)
    my_rank = lax.dynamic_index_in_dim(rank, ping_index, 0, keepdims=False)
    leaving = (mine[None, None, :] == place[:, None, None]) & (my_rank[None, None, :] == pair[None, :, None])
    table = jnp.sum(jnp.where(leaving, place[None, None, :] + 1, 0), 2) - 1
    coming = (owners[:, None, :] == ping_index) & (rank[:, None, :] == pair[None, :, None])
    target = slots * 2 + place[None, :] % 2
    ids = jnp.sum(jnp.where(coming, target[:, None, :] + 1, 0), 2) - 1
    return table.reshape(32), ids.reshape(32)


def on_device(echoes, replica, steering, angle_weights, range_weights, range_offsets, merge_owner, merge_slot):
    ping_index = lax.axis_index("ping")
    x = echoes.reshape(16, 8, 2, 64, 128).transpose(0, 1, 3, 2, 4).reshape(16, 8, 128, 128)
    taps = jnp.roll(jnp.flip(replica, 2), 1, 2).astype(jnp.float32)
    table, ids = routing(merge_owner, merge_slot, ping_index)
    angle = angle_matrix(steering, angle_weights)
    width = 8 // CHUNKS
    arrived = []
    for chunk in range(CHUNKS):
        sent = compress(x, taps, width * chunk, width)
        band_tile = lax.all_to_all(sent, "band", split_axis=0, concat_axis=0, tiled=True)
        blocks = band_tile.reshape(16, 8, width * 16, 128)
        outgoing = pack(table, blocks)
        arrived.append(lax.all_to_all(outgoing, "ping", split_axis=0, concat_axis=0, tiled=True))
    merged = form_images(ids, range_offsets, arrived, angle, range_weights)
    return merged.reshape(8, 2, 128, 1024)


def solution(mesh):
    placed = (
        P(("ping", "band"), None, None, None),
        P(),
        P(),
        P(),
        P("band", None, None),
        P("band"),
        P(),
        P(),
    )
    return jax.shard_map(
        on_device,
        mesh=mesh,
        in_specs=placed,
        out_specs=P("ping", None, None, "band"),
        check_vma=False,
    )
```

```python
import functools

import jax
import jax.numpy as jnp
from jax import lax
from jax.experimental import pallas as pl
from jax.experimental.pallas import tpu as pltpu
from jax.sharding import PartitionSpec as P

CHUNKS = 1
VMEM_LIMIT = 56 * 1024 * 1024


def compress_kernel(x_ref, taps_ref, out_ref):
    row = lax.broadcasted_iota(jnp.int32, (128, 128), 0)
    col = lax.broadcasted_iota(jnp.int32, (128, 128), 1)
    lower, upper = [], []
    for part in range(2):
        line = jnp.broadcast_to(taps_ref[0, part : part + 1, :], (128, 128))
        circulant = pltpu.roll(line, 0, 1, stride=1, stride_axis=0)
        lower.append(jnp.where(row >= col, circulant, 0.0))
        upper.append(jnp.where(row < col, circulant, 0.0))
    weights = jnp.concatenate(
        [
            jnp.concatenate([lower[0], -lower[1]], 1),
            jnp.concatenate([lower[1], lower[0]], 1),
            jnp.concatenate([upper[0], -upper[1]], 1),
            jnp.concatenate([upper[1], upper[0]], 1),
        ],
        0,
    ).astype(jnp.bfloat16)
    wanted = (row & 7) * 16 + ((row >> 3) & 7) * 2 + (row >> 6)
    permute = (wanted == col).astype(jnp.float32).astype(jnp.bfloat16)
    for block in range(2):
        real, imag = [], []
        for tile in range(8):
            rows = x_ref[8 * block : 8 * block + 8, 0, 16 * tile : 16 * tile + 16, :]
            moved = jnp.dot(permute, rows.reshape(128, 128), preferred_element_type=jnp.float32)
            real.append(moved[:64])
            imag.append(moved[64:])
        real = jnp.concatenate(real, 0)
        imag = jnp.concatenate(imag, 0)
        nothing = jnp.zeros((8, 128), jnp.float32)
        real_next = jnp.concatenate([real[8:], nothing], 0)
        imag_next = jnp.concatenate([imag[8:], nothing], 0)
        stacked = jnp.concatenate([real, imag, real_next, imag_next], 1).astype(jnp.bfloat16)
        product = jnp.dot(stacked, weights, preferred_element_type=jnp.float32)
        product = product.reshape(64, 8, 256)
        product = jnp.concatenate([product[:, :, :128], product[:, :, 128:]], 1)
        out_ref[:, block, :, 0] = product.astype(jnp.bfloat16).reshape(8, 8, 16, 128)


def compress(x, taps, first, count):
    return pl.pallas_call(
        compress_kernel,
        grid=(count,),
        in_specs=[
            pl.BlockSpec((16, 1, 128, 128), lambda i: (0, first + i, 0, 0)),
            pl.BlockSpec((1, 2, 128), lambda i: (first + i, 0, 0)),
        ],
        out_specs=pl.BlockSpec((8, 2, 8, 1, 16, 128), lambda i: (0, 0, 0, i, 0, 0)),
        out_shape=jax.ShapeDtypeStruct((8, 2, 8, count, 16, 128), jnp.bfloat16),
        compiler_params=pltpu.CompilerParams(vmem_limit_bytes=VMEM_LIMIT),
        name="compress",
    )(x, taps)


def pack_kernel(table_ref, source_ref, out_ref, held, in_sems, out_sems):
    def fetch(block):
        return pltpu.make_async_copy(source_ref.at[block], held.at[block], in_sems.at[block])

    def send(block):
        slot = jnp.maximum(table_ref[block], 0)
        return pltpu.make_async_copy(held.at[block], out_ref.at[slot], out_sems.at[block])

    for block in range(16):
        fetch(block).start()
    for block in range(16):
        fetch(block).wait()

        @pl.when(table_ref[block] >= 0)
        def _():
            send(block).start()

    for block in range(16):

        @pl.when(table_ref[block] >= 0)
        def _():
            send(block).wait()


def pack(table, source):
    return pl.pallas_call(
        pack_kernel,
        grid_spec=pltpu.PrefetchScalarGridSpec(
            num_scalar_prefetch=1,
            grid=(1,),
            in_specs=[pl.BlockSpec(memory_space=pl.ANY)],
            out_specs=pl.BlockSpec(memory_space=pl.ANY),
            scratch_shapes=[
                pltpu.VMEM(source.shape, source.dtype),
                pltpu.SemaphoreType.DMA((16,)),
                pltpu.SemaphoreType.DMA((16,)),
            ],
        ),
        out_shape=jax.ShapeDtypeStruct((32,) + source.shape[1:], source.dtype),
        compiler_params=pltpu.CompilerParams(vmem_limit_bytes=VMEM_LIMIT),
        name="pack",
    )(table, source)


def image_kernel(chunks, ids_ref, offsets_ref, *refs):
    arrived = refs[:chunks]
    angle_ref, range_ref, out_ref, total, turned = refs[chunks:]
    step = pl.program_id(0)
    height = 128 // chunks

    @pl.when(step < 8)
    def _():
        total[...] = jnp.zeros_like(total)

        def add(slot, carry):
            target = ids_ref[slot]

            @pl.when(target >= 0)
            def _():
                for chunk in range(chunks):
                    rows = pl.ds(chunk * height, height)
                    total[target, rows, :] += arrived[chunk][slot, 0].astype(jnp.float32)

            return carry

        lax.fori_loop(0, 32, add, 0)
        angle = angle_ref[...]
        for image in range(8):
            both = total[2 * image : 2 * image + 2].reshape(256, 128).astype(jnp.bfloat16)
            product = jnp.dot(angle, both, preferred_element_type=jnp.float32)
            turned[step, 256 * image : 256 * image + 256, :] = product.astype(jnp.bfloat16)

    @pl.when(step >= 8)
    def _():
        start = offsets_ref[jnp.maximum(step - 8, 0)]
        for half in range(2):
            rows = pl.ds(1024 * half, 1024)
            slab = jnp.concatenate([turned[start + i, rows, :] for i in range(3)], 1)
            product = jnp.dot(slab, range_ref[0], preferred_element_type=jnp.float32)
            out_ref[rows, :] = product.astype(jnp.bfloat16)


def form_images(ids, offsets, arrived, angle, range_weights):
    chunks = len(arrived)
    height = 128 // chunks
    return pl.pallas_call(
        functools.partial(image_kernel, chunks),
        grid_spec=pltpu.PrefetchScalarGridSpec(
            num_scalar_prefetch=2,
            grid=(16,),
            in_specs=[pl.BlockSpec((32, 1, height, 128), lambda s, *_: (0, jnp.minimum(s, 7), 0, 0))]
            * chunks
            + [
                pl.BlockSpec((256, 256), lambda s, *_: (0, 0)),
                pl.BlockSpec((1, 384, 128), lambda s, *_: (jnp.maximum(s - 8, 0), 0, 0)),
            ],
            out_specs=pl.BlockSpec((2048, 128), lambda s, *_: (0, jnp.maximum(s - 8, 0))),
            scratch_shapes=[
                pltpu.VMEM((16, 128, 128), jnp.float32),
                pltpu.VMEM((8, 2048, 128), jnp.bfloat16),
            ],
        ),
        out_shape=jax.ShapeDtypeStruct((2048, 1024), jnp.bfloat16),
        compiler_params=pltpu.CompilerParams(vmem_limit_bytes=VMEM_LIMIT),
        name="form_images",
    )(ids, offsets, *arrived, angle, range_weights)


def angle_matrix(steering, angle_weights):
    both = jnp.einsum("pya,sae->pyse", angle_weights, steering, preferred_element_type=jnp.float32)
    real, imag = both[:, :, 0], both[:, :, 1]
    full = jnp.stack([jnp.stack([real, -imag], 2), jnp.stack([imag, real], 2)], 0)
    full = full.astype(jnp.bfloat16).reshape(2, 2, 128, 2, 8, 8)
    return full.transpose(0, 2, 1, 5, 3, 4).reshape(256, 256)


def routing(merge_owner, merge_slot, ping_index):
    owners = merge_owner.reshape(16, 16)
    slots = merge_slot.reshape(16, 16)
    place = jnp.arange(16, dtype=jnp.int32)
    same = (owners[:, :, None] == owners[:, None, :]) & (place[None, :, None] > place[None, None, :])
    rank = jnp.sum(same.astype(jnp.int32), 2)
    leaving = jnp.where(owners >= 0, owners * 2 + rank, -1)
    table = lax.dynamic_index_in_dim(leaving, ping_index, 0, keepdims=False)
    pair = jnp.arange(2, dtype=jnp.int32)
    coming = (owners[:, None, :] == ping_index) & (rank[:, None, :] == pair[None, :, None])
    target = slots * 2 + place[None, :] % 2
    ids = jnp.sum(jnp.where(coming, target[:, None, :] + 1, 0), 2) - 1
    return table, ids.reshape(32)


def on_device(echoes, replica, steering, angle_weights, range_weights, range_offsets, merge_owner, merge_slot):
    ping_index = lax.axis_index("ping")
    x = echoes.reshape(16, 8, 2, 64, 128).transpose(0, 1, 3, 2, 4).reshape(16, 8, 128, 128)
    taps = jnp.roll(jnp.flip(replica, 2), 1, 2).astype(jnp.float32)
    table, ids = routing(merge_owner, merge_slot, ping_index)
    angle = angle_matrix(steering, angle_weights)
    width = 8 // CHUNKS
    arrived = []
    for chunk in range(CHUNKS):
        sent = compress(x, taps, width * chunk, width)
        band_tile = lax.all_to_all(sent, "band", split_axis=0, concat_axis=0, tiled=True)
        blocks = band_tile.reshape(16, 8, width * 16, 128)
        outgoing = pack(table, blocks)
        arrived.append(lax.all_to_all(outgoing, "ping", split_axis=0, concat_axis=0, tiled=True))
    merged = form_images(ids, range_offsets, arrived, angle, range_weights)
    return merged.reshape(8, 2, 128, 1024)


def solution(mesh):
    placed = (
        P(("ping", "band"), None, None, None),
        P(),
        P(),
        P(),
        P("band", None, None),
        P("band"),
        P(),
        P(),
    )
    return jax.shard_map(
        on_device,
        mesh=mesh,
        in_specs=placed,
        out_specs=P("ping", None, None, "band"),
        check_vma=False,
    )
```

```python
import functools

import jax
import jax.numpy as jnp
from jax import lax
from jax.experimental import pallas as pl
from jax.experimental.pallas import tpu as pltpu
from jax.sharding import PartitionSpec as P

CHUNKS = 1
VMEM_LIMIT = 56 * 1024 * 1024


def compress_kernel(x_ref, taps_ref, out_ref):
    row = lax.broadcasted_iota(jnp.int32, (128, 128), 0)
    col = lax.broadcasted_iota(jnp.int32, (128, 128), 1)
    lower, upper = [], []
    for part in range(2):
        line = jnp.broadcast_to(taps_ref[0, part : part + 1, :], (128, 128))
        circulant = pltpu.roll(line, 0, 1, stride=1, stride_axis=0)
        lower.append(jnp.where(row >= col, circulant, 0.0))
        upper.append(jnp.where(row < col, circulant, 0.0))
    weights = jnp.concatenate(
        [
            jnp.concatenate([lower[0], -lower[1]], 1),
            jnp.concatenate([lower[1], lower[0]], 1),
            jnp.concatenate([upper[0], -upper[1]], 1),
            jnp.concatenate([upper[1], upper[0]], 1),
        ],
        0,
    ).astype(jnp.bfloat16)
    wanted = (row & 7) * 16 + ((row >> 3) & 7) * 2 + (row >> 6)
    permute = (wanted == col).astype(jnp.float32).astype(jnp.bfloat16)
    for block in range(2):
        real, imag = [], []
        for tile in range(8):
            rows = x_ref[8 * block : 8 * block + 8, 0, 16 * tile : 16 * tile + 16, :]
            moved = jnp.dot(permute, rows.reshape(128, 128), preferred_element_type=jnp.float32)
            real.append(moved[:64])
            imag.append(moved[64:])
        real = jnp.concatenate(real, 0)
        imag = jnp.concatenate(imag, 0)
        nothing = jnp.zeros((8, 128), jnp.float32)
        real_next = jnp.concatenate([real[8:], nothing], 0)
        imag_next = jnp.concatenate([imag[8:], nothing], 0)
        stacked = jnp.concatenate([real, imag, real_next, imag_next], 1).astype(jnp.bfloat16)
        product = jnp.dot(stacked, weights, preferred_element_type=jnp.float32)
        product = product.reshape(64, 8, 256)
        product = jnp.concatenate([product[:, :, :128], product[:, :, 128:]], 1)
        out_ref[:, block, :, 0] = product.astype(jnp.bfloat16).reshape(8, 8, 16, 128)


def compress(x, taps, first, count):
    return pl.pallas_call(
        compress_kernel,
        grid=(count,),
        in_specs=[
            pl.BlockSpec((16, 1, 128, 128), lambda i: (0, first + i, 0, 0)),
            pl.BlockSpec((1, 2, 128), lambda i: (first + i, 0, 0)),
        ],
        out_specs=pl.BlockSpec((8, 2, 8, 1, 16, 128), lambda i: (0, 0, 0, i, 0, 0)),
        out_shape=jax.ShapeDtypeStruct((8, 2, 8, count, 16, 128), jnp.bfloat16),
        compiler_params=pltpu.CompilerParams(vmem_limit_bytes=VMEM_LIMIT),
        name="compress",
    )(x, taps)


def pack_kernel(table_ref, source_ref, out_ref, held, in_sems, out_sems):
    def fetch(block):
        return pltpu.make_async_copy(source_ref.at[block], held.at[block], in_sems.at[block])

    def send(block):
        slot = jnp.maximum(table_ref[block], 0)
        return pltpu.make_async_copy(held.at[block], out_ref.at[slot], out_sems.at[block])

    for block in range(16):
        fetch(block).start()
    for block in range(16):
        fetch(block).wait()

        @pl.when(table_ref[block] >= 0)
        def _():
            send(block).start()

    for block in range(16):

        @pl.when(table_ref[block] >= 0)
        def _():
            send(block).wait()


def pack(table, source):
    return pl.pallas_call(
        pack_kernel,
        grid_spec=pltpu.PrefetchScalarGridSpec(
            num_scalar_prefetch=1,
            grid=(1,),
            in_specs=[pl.BlockSpec(memory_space=pl.ANY)],
            out_specs=pl.BlockSpec(memory_space=pl.ANY),
            scratch_shapes=[
                pltpu.VMEM(source.shape, source.dtype),
                pltpu.SemaphoreType.DMA((16,)),
                pltpu.SemaphoreType.DMA((16,)),
            ],
        ),
        out_shape=jax.ShapeDtypeStruct((32,) + source.shape[1:], source.dtype),
        compiler_params=pltpu.CompilerParams(vmem_limit_bytes=VMEM_LIMIT),
        name="pack",
    )(table, source)


def image_kernel(chunks, ids_ref, offsets_ref, *refs):
    arrived = refs[:chunks]
    angle_ref, range_ref, out_ref, total, turned, angle = refs[chunks:]
    step = pl.program_id(0)
    height = 128 // chunks

    @pl.when(step == 0)
    def _():
        angle[...] = jnp.transpose(angle_ref[...].astype(jnp.float32)).astype(jnp.bfloat16)

    @pl.when(step < 8)
    def _():
        total[...] = jnp.zeros_like(total)

        def add(slot, carry):
            target = ids_ref[slot]

            @pl.when(target >= 0)
            def _():
                for chunk in range(chunks):
                    rows = pl.ds(chunk * height, height)
                    total[target, rows, :] += arrived[chunk][slot, 0].astype(jnp.float32)

            return carry

        lax.fori_loop(0, 32, add, 0)
        for image in range(8):
            both = total[2 * image : 2 * image + 2].reshape(256, 128).astype(jnp.bfloat16)
            product = jnp.dot(angle[...], both, preferred_element_type=jnp.float32)
            turned[step, 256 * image : 256 * image + 256, :] = product.astype(jnp.bfloat16)

    @pl.when(step >= 8)
    def _():
        start = offsets_ref[jnp.maximum(step - 8, 0)]
        for half in range(2):
            rows = pl.ds(1024 * half, 1024)
            slab = jnp.concatenate([turned[start + i, rows, :] for i in range(3)], 1)
            product = jnp.dot(slab, range_ref[0], preferred_element_type=jnp.float32)
            out_ref[rows, :] = product.astype(jnp.bfloat16)


def form_images(ids, offsets, arrived, angle, range_weights):
    chunks = len(arrived)
    height = 128 // chunks
    return pl.pallas_call(
        functools.partial(image_kernel, chunks),
        grid_spec=pltpu.PrefetchScalarGridSpec(
            num_scalar_prefetch=2,
            grid=(16,),
            in_specs=[pl.BlockSpec((32, 1, height, 128), lambda s, *_: (0, jnp.minimum(s, 7), 0, 0))]
            * chunks
            + [
                pl.BlockSpec((256, 256), lambda s, *_: (0, 0)),
                pl.BlockSpec((1, 384, 128), lambda s, *_: (jnp.maximum(s - 8, 0), 0, 0)),
            ],
            out_specs=pl.BlockSpec((2048, 128), lambda s, *_: (0, jnp.maximum(s - 8, 0))),
            scratch_shapes=[
                pltpu.VMEM((16, 128, 128), jnp.float32),
                pltpu.VMEM((8, 2048, 128), jnp.bfloat16),
                pltpu.VMEM((256, 256), jnp.bfloat16),
            ],
        ),
        out_shape=jax.ShapeDtypeStruct((2048, 1024), jnp.bfloat16),
        compiler_params=pltpu.CompilerParams(vmem_limit_bytes=VMEM_LIMIT),
        name="form_images",
    )(ids, offsets, *arrived, angle, range_weights)


def angle_matrix(steering, angle_weights):
    both = jnp.einsum("pya,sae->pyse", angle_weights, steering, preferred_element_type=jnp.float32)
    real, imag = both[:, :, 0], both[:, :, 1]
    full = jnp.stack([jnp.stack([real, -imag], 2), jnp.stack([imag, real], 2)], 0)
    full = full.astype(jnp.bfloat16).reshape(2, 2, 128, 2, 8, 8)
    return full.transpose(1, 5, 3, 4, 0, 2).reshape(256, 256)


def routing(merge_owner, merge_slot, ping_index):
    owners = merge_owner.reshape(16, 16)
    slots = merge_slot.reshape(16, 16)
    place = jnp.arange(16, dtype=jnp.int32)
    same = (owners[:, :, None] == owners[:, None, :]) & (place[None, :, None] > place[None, None, :])
    rank = jnp.sum(same.astype(jnp.int32), 2)
    leaving = jnp.where(owners >= 0, owners * 2 + rank, -1)
    table = lax.dynamic_index_in_dim(leaving, ping_index, 0, keepdims=False)
    pair = jnp.arange(2, dtype=jnp.int32)
    coming = (owners[:, None, :] == ping_index) & (rank[:, None, :] == pair[None, :, None])
    target = slots * 2 + place[None, :] % 2
    ids = jnp.sum(jnp.where(coming, target[:, None, :] + 1, 0), 2) - 1
    return table, ids.reshape(32)


def on_device(echoes, replica, steering, angle_weights, range_weights, range_offsets, merge_owner, merge_slot):
    ping_index = lax.axis_index("ping")
    x = echoes.reshape(16, 8, 2, 64, 128).transpose(0, 1, 3, 2, 4).reshape(16, 8, 128, 128)
    taps = jnp.roll(jnp.flip(replica, 2), 1, 2).astype(jnp.float32)
    table, ids = routing(merge_owner, merge_slot, ping_index)
    angle = angle_matrix(steering, angle_weights)
    width = 8 // CHUNKS
    arrived = []
    for chunk in range(CHUNKS):
        sent = compress(x, taps, width * chunk, width)
        sent, table, ids, angle = lax.optimization_barrier((sent, table, ids, angle))
        band_tile = lax.all_to_all(sent, "band", split_axis=0, concat_axis=0, tiled=True)
        blocks = band_tile.reshape(16, 8, width * 16, 128)
        outgoing = pack(table, blocks)
        arrived.append(lax.all_to_all(outgoing, "ping", split_axis=0, concat_axis=0, tiled=True))
    merged = form_images(ids, range_offsets, arrived, angle, range_weights)
    return merged.reshape(8, 2, 128, 1024)


def solution(mesh):
    placed = (
        P(("ping", "band"), None, None, None),
        P(),
        P(),
        P(),
        P("band", None, None),
        P("band"),
        P(),
        P(),
    )
    return jax.shard_map(
        on_device,
        mesh=mesh,
        in_specs=placed,
        out_specs=P("ping", None, None, "band"),
        check_vma=False,
    )
```

```python
import functools

import jax
import jax.numpy as jnp
from jax import lax
from jax.experimental import pallas as pl
from jax.experimental.pallas import tpu as pltpu
from jax.sharding import PartitionSpec as P

SPLIT = 4
VMEM_LIMIT = 56 * 1024 * 1024


def compress_kernel(relative, band_ref, x_ref, taps_ref, *refs):
    row = lax.broadcasted_iota(jnp.int32, (128, 128), 0)
    col = lax.broadcasted_iota(jnp.int32, (128, 128), 1)
    lower, upper = [], []
    for part in range(2):
        line = jnp.broadcast_to(taps_ref[0, part : part + 1, :], (128, 128))
        circulant = pltpu.roll(line, 0, 1, stride=1, stride_axis=0)
        lower.append(jnp.where(row >= col, circulant, 0.0))
        upper.append(jnp.where(row < col, circulant, 0.0))
    weights = jnp.concatenate(
        [
            jnp.concatenate([lower[0], -lower[1]], 1),
            jnp.concatenate([lower[1], lower[0]], 1),
            jnp.concatenate([upper[0], -upper[1]], 1),
            jnp.concatenate([upper[1], upper[0]], 1),
        ],
        0,
    ).astype(jnp.bfloat16)
    wanted = (row & 7) * 16 + ((row >> 3) & 7) * 2 + (row >> 6)
    permute = (wanted == col).astype(jnp.float32).astype(jnp.bfloat16)
    for block in range(2):
        real, imag = [], []
        for tile in range(8):
            rows = x_ref[8 * block : 8 * block + 8, 0, 16 * tile : 16 * tile + 16, :]
            moved = jnp.dot(permute, rows.reshape(128, 128), preferred_element_type=jnp.float32)
            real.append(moved[:64])
            imag.append(moved[64:])
        real = jnp.concatenate(real, 0)
        imag = jnp.concatenate(imag, 0)
        nothing = jnp.zeros((8, 128), jnp.float32)
        real_next = jnp.concatenate([real[8:], nothing], 0)
        imag_next = jnp.concatenate([imag[8:], nothing], 0)
        stacked = jnp.concatenate([real, imag, real_next, imag_next], 1).astype(jnp.bfloat16)
        product = jnp.dot(stacked, weights, preferred_element_type=jnp.float32)
        product = product.reshape(64, 8, 256)
        product = jnp.concatenate([product[:, :, :128], product[:, :, 128:]], 1)
        product = product.astype(jnp.bfloat16).reshape(8, 8, 16, 128)
        if not relative:
            refs[0][:, block, :, 0] = product
            continue
        held = refs[4]
        held[...] = product
        for step in range(4):
            for other in range(2):
                refs[step][other, block, :, 0] = held[band_at(band_ref[0], step, other)]


def band_at(band, step, other):
    return ((band >> 1) + step) % 4 * 2 + ((band & 1) + other) % 2


def compress(band, x, taps, first, count, relative):
    lead, outs = (2, 4) if relative else (8, 1)
    return pl.pallas_call(
        functools.partial(compress_kernel, relative),
        grid_spec=pltpu.PrefetchScalarGridSpec(
            num_scalar_prefetch=1,
            grid=(count,),
            in_specs=[
                pl.BlockSpec((16, 1, 128, 128), lambda i, *_: (0, first + i, 0, 0)),
                pl.BlockSpec((1, 2, 128), lambda i, *_: (first + i, 0, 0)),
            ],
            out_specs=[pl.BlockSpec((lead, 2, 8, 1, 16, 128), lambda i, *_: (0, 0, 0, i, 0, 0))] * outs,
            scratch_shapes=[pltpu.VMEM((8, 8, 16, 128), jnp.bfloat16)] * relative,
        ),
        out_shape=[jax.ShapeDtypeStruct((lead, 2, 8, count, 16, 128), jnp.bfloat16)] * outs,
        compiler_params=pltpu.CompilerParams(vmem_limit_bytes=VMEM_LIMIT),
        name="compress_relative" if relative else "compress",
    )(band, x, taps)


def pack_kernel(relative, table_ref, band_ref, *refs):
    sources, (out_ref, held, in_sems, out_sems) = refs[:-4], refs[-4:]

    def source(block):
        if not relative:
            return sources[0].at[block // 2, block % 2]
        step, other = block // 4, block // 2 % 2
        return sources[4].at[step, block % 2] if other else sources[step].at[0, block % 2]

    def name(block):
        if not relative:
            return block
        return 2 * band_at(band_ref[0], 4 - block // 4, block // 2 % 2) + block % 2

    def fetch(block):
        return pltpu.make_async_copy(source(block), held.at[block], in_sems.at[block])

    def send(block):
        slot = jnp.maximum(table_ref[name(block)], 0)
        return pltpu.make_async_copy(held.at[block], out_ref.at[slot], out_sems.at[block])

    for block in range(16):
        fetch(block).start()
    for block in range(16):
        fetch(block).wait()

        @pl.when(table_ref[name(block)] >= 0)
        def _():
            send(block).start()

    for block in range(16):

        @pl.when(table_ref[name(block)] >= 0)
        def _():
            send(block).wait()


def pack(table, band, *sources):
    shape, kind = sources[0].shape[2:], sources[0].dtype
    return pl.pallas_call(
        functools.partial(pack_kernel, len(sources) > 1),
        grid_spec=pltpu.PrefetchScalarGridSpec(
            num_scalar_prefetch=2,
            grid=(1,),
            in_specs=[pl.BlockSpec(memory_space=pl.ANY)] * len(sources),
            out_specs=pl.BlockSpec(memory_space=pl.ANY),
            scratch_shapes=[
                pltpu.VMEM((16,) + shape, kind),
                pltpu.SemaphoreType.DMA((16,)),
                pltpu.SemaphoreType.DMA((16,)),
            ],
        ),
        out_shape=jax.ShapeDtypeStruct((32,) + shape, kind),
        compiler_params=pltpu.CompilerParams(vmem_limit_bytes=VMEM_LIMIT),
        name="pack",
    )(table, band, *sources)


def image_kernel(chunks, ids_ref, offsets_ref, *refs):
    arrived = refs[:chunks]
    angle_ref, range_ref, out_ref, total, turned, angle = refs[chunks:]
    step = pl.program_id(0)
    heights = [part.shape[2] for part in arrived]

    @pl.when(step == 0)
    def _():
        angle[...] = jnp.transpose(angle_ref[...].astype(jnp.float32)).astype(jnp.bfloat16)

    @pl.when(step < 8)
    def _():
        total[...] = jnp.zeros_like(total)

        def add(slot, carry):
            target = ids_ref[slot]

            @pl.when(target >= 0)
            def _():
                for chunk in range(chunks):
                    rows = pl.ds(sum(heights[:chunk]), heights[chunk])
                    total[target, rows, :] += arrived[chunk][slot, 0].astype(jnp.float32)

            return carry

        lax.fori_loop(0, 32, add, 0)
        for image in range(8):
            both = total[2 * image : 2 * image + 2].reshape(256, 128).astype(jnp.bfloat16)
            product = jnp.dot(angle[...], both, preferred_element_type=jnp.float32)
            turned[step, 256 * image : 256 * image + 256, :] = product.astype(jnp.bfloat16)

    @pl.when(step >= 8)
    def _():
        start = offsets_ref[jnp.maximum(step - 8, 0)]
        for half in range(2):
            rows = pl.ds(1024 * half, 1024)
            slab = jnp.concatenate([turned[start + i, rows, :] for i in range(3)], 1)
            product = jnp.dot(slab, range_ref[0], preferred_element_type=jnp.float32)
            out_ref[rows, :] = product.astype(jnp.bfloat16)


def form_images(ids, offsets, arrived, angle, range_weights):
    chunks = len(arrived)
    return pl.pallas_call(
        functools.partial(image_kernel, chunks),
        grid_spec=pltpu.PrefetchScalarGridSpec(
            num_scalar_prefetch=2,
            grid=(16,),
            in_specs=[
                pl.BlockSpec((32, 1, part.shape[2], 128), lambda s, *_: (0, jnp.minimum(s, 7), 0, 0))
                for part in arrived
            ]
            + [
                pl.BlockSpec((256, 256), lambda s, *_: (0, 0)),
                pl.BlockSpec((1, 384, 128), lambda s, *_: (jnp.maximum(s - 8, 0), 0, 0)),
            ],
            out_specs=pl.BlockSpec((2048, 128), lambda s, *_: (0, jnp.maximum(s - 8, 0))),
            scratch_shapes=[
                pltpu.VMEM((16, 128, 128), jnp.float32),
                pltpu.VMEM((8, 2048, 128), jnp.bfloat16),
                pltpu.VMEM((256, 256), jnp.bfloat16),
            ],
        ),
        out_shape=jax.ShapeDtypeStruct((2048, 1024), jnp.bfloat16),
        compiler_params=pltpu.CompilerParams(vmem_limit_bytes=VMEM_LIMIT),
        name="form_images",
    )(ids, offsets, *arrived, angle, range_weights)


def angle_matrix(steering, angle_weights):
    both = jnp.einsum("pya,sae->pyse", angle_weights, steering, preferred_element_type=jnp.float32)
    real, imag = both[:, :, 0], both[:, :, 1]
    full = jnp.stack([jnp.stack([real, -imag], 2), jnp.stack([imag, real], 2)], 0)
    full = full.astype(jnp.bfloat16).reshape(2, 2, 128, 2, 8, 8)
    return full.transpose(1, 5, 3, 4, 0, 2).reshape(256, 256)


def routing(merge_owner, merge_slot, ping_index):
    owners = merge_owner.reshape(16, 16)
    slots = merge_slot.reshape(16, 16)
    place = jnp.arange(16, dtype=jnp.int32)
    same = (owners[:, :, None] == owners[:, None, :]) & (place[None, :, None] > place[None, None, :])
    rank = jnp.sum(same.astype(jnp.int32), 2)
    leaving = jnp.where(owners >= 0, owners * 2 + rank, -1)
    table = lax.dynamic_index_in_dim(leaving, ping_index, 0, keepdims=False)
    pair = jnp.arange(2, dtype=jnp.int32)
    coming = (owners[:, None, :] == ping_index) & (rank[:, None, :] == pair[None, :, None])
    target = slots * 2 + place[None, :] % 2
    ids = jnp.sum(jnp.where(coming, target[:, None, :] + 1, 0), 2) - 1
    return table, ids.reshape(32)


def to_owners(some, outgoing):
    def exchange(blocks):
        return lax.all_to_all(blocks, "ping", split_axis=0, concat_axis=0, tiled=True)

    return lax.cond(some, exchange, lambda blocks: blocks, outgoing)


def flat(part):
    return part.reshape(part.shape[:3] + (-1, 128))


def ring_step(step, other):
    return [(band, ((band // 2 + step) % 4) * 2 + (band + other) % 2) for band in range(8)]


def on_device(echoes, replica, steering, angle_weights, range_weights, range_offsets, merge_owner, merge_slot):
    ping_index = lax.axis_index("ping")
    x = echoes.reshape(16, 8, 2, 64, 128).transpose(0, 1, 3, 2, 4).reshape(16, 8, 128, 128)
    taps = jnp.roll(jnp.flip(replica, 2), 1, 2).astype(jnp.float32)
    table, ids = routing(merge_owner, merge_slot, ping_index)
    angle = angle_matrix(steering, angle_weights)
    band_index = lax.axis_index("band")
    band = band_index.reshape(1).astype(jnp.int32)
    (sent,) = compress(band, x, taps, 0, SPLIT, False)
    sent, x, table, ids, angle = lax.optimization_barrier((sent, x, table, ids, angle))
    band_tile = lax.all_to_all(sent, "band", split_axis=0, concat_axis=0, tiled=True)
    band_tile, x = lax.optimization_barrier((band_tile, x))
    ring = compress(band, x, taps, SPLIT, 8 - SPLIT, True)
    outgoing = pack(table, band, flat(band_tile))
    outgoing, *ring = lax.optimization_barrier((outgoing, *ring))
    moved = [ring[0]] + [lax.ppermute(ring[step], "band", ring_step(step, 0)) for step in (1, 2, 3)]
    first = to_owners(jnp.any(merge_owner >= 0), outgoing)
    first, *moved = lax.optimization_barrier((first, *moved))
    others = lax.ppermute(jnp.stack([part[1] for part in moved]), "band", ring_step(0, 1))
    outgoing = pack(table, band, *[flat(part) for part in moved], flat(others))
    second = lax.all_to_all(outgoing, "ping", split_axis=0, concat_axis=0, tiled=True)
    arrived = [first, second]
    merged = form_images(ids, range_offsets, arrived, angle, range_weights)
    return merged.reshape(8, 2, 128, 1024)


def solution(mesh):
    placed = (
        P(("ping", "band"), None, None, None),
        P(),
        P(),
        P(),
        P("band", None, None),
        P("band"),
        P(),
        P(),
    )
    return jax.shard_map(
        on_device,
        mesh=mesh,
        in_specs=placed,
        out_specs=P("ping", None, None, "band"),
        check_vma=False,
    )
```

```python
import functools

import jax
import jax.numpy as jnp
from jax import lax
from jax.experimental import pallas as pl
from jax.experimental.pallas import tpu as pltpu
from jax.sharding import PartitionSpec as P

SPLIT = 3
VMEM_LIMIT = 56 * 1024 * 1024


def compress_kernel(relative, band_ref, x_ref, taps_ref, *refs):
    row = lax.broadcasted_iota(jnp.int32, (128, 128), 0)
    col = lax.broadcasted_iota(jnp.int32, (128, 128), 1)
    lower, upper = [], []
    for part in range(2):
        line = jnp.broadcast_to(taps_ref[0, part : part + 1, :].astype(jnp.float32), (128, 128))
        circulant = jnp.transpose(pltpu.roll(line, 0, 1, stride=1, stride_axis=0))
        lower.append(jnp.where(row >= col, circulant, 0.0))
        upper.append(jnp.where(row < col, circulant, 0.0))
    weights = jnp.concatenate(
        [
            jnp.concatenate([lower[0], -lower[1]], 1),
            jnp.concatenate([lower[1], lower[0]], 1),
            jnp.concatenate([upper[0], -upper[1]], 1),
            jnp.concatenate([upper[1], upper[0]], 1),
        ],
        0,
    ).astype(jnp.bfloat16)
    wanted = (row & 7) * 16 + ((row >> 3) & 7) * 2 + (row >> 6)
    permute = (wanted == col).astype(jnp.float32).astype(jnp.bfloat16)
    for block in range(2):
        real, imag = [], []
        for tile in range(8):
            rows = x_ref[8 * block : 8 * block + 8, 0, 16 * tile : 16 * tile + 16, :]
            moved = jnp.dot(permute, rows.reshape(128, 128), preferred_element_type=jnp.float32)
            real.append(moved[:64])
            imag.append(moved[64:])
        real = jnp.concatenate(real, 0)
        imag = jnp.concatenate(imag, 0)
        nothing = jnp.zeros((8, 128), jnp.float32)
        real_next = jnp.concatenate([real[8:], nothing], 0)
        imag_next = jnp.concatenate([imag[8:], nothing], 0)
        stacked = jnp.concatenate([real, imag, real_next, imag_next], 1).astype(jnp.bfloat16)
        product = jnp.dot(stacked, weights, preferred_element_type=jnp.float32)
        product = product.reshape(64, 8, 256)
        product = jnp.concatenate([product[:, :, :128], product[:, :, 128:]], 1)
        product = product.astype(jnp.bfloat16).reshape(8, 8, 16, 128)
        if not relative:
            refs[0][:, block, :, 0] = product
            continue
        held = refs[4]
        held[...] = product
        for step in range(4):
            for other in range(2):
                refs[step][other, block, :, 0] = held[band_at(band_ref[0], step, other)]


def band_at(band, step, other):
    return ((band >> 1) + step) % 4 * 2 + ((band & 1) + other) % 2


def compress(band, x, taps, first, count, relative):
    lead, outs = (2, 4) if relative else (8, 1)
    return pl.pallas_call(
        functools.partial(compress_kernel, relative),
        grid_spec=pltpu.PrefetchScalarGridSpec(
            num_scalar_prefetch=1,
            grid=(count,),
            in_specs=[
                pl.BlockSpec((16, 1, 128, 128), lambda i, *_: (0, first + i, 0, 0)),
                pl.BlockSpec((1, 2, 128), lambda i, *_: (first + i, 0, 0)),
            ],
            out_specs=[pl.BlockSpec((lead, 2, 8, 1, 16, 128), lambda i, *_: (0, 0, 0, i, 0, 0))] * outs,
            scratch_shapes=[pltpu.VMEM((8, 8, 16, 128), jnp.bfloat16)] * relative,
        ),
        out_shape=[jax.ShapeDtypeStruct((lead, 2, 8, count, 16, 128), jnp.bfloat16)] * outs,
        compiler_params=pltpu.CompilerParams(vmem_limit_bytes=VMEM_LIMIT),
        name="compress_relative" if relative else "compress",
    )(band, x, taps)


def pack_kernel(relative, table_ref, band_ref, *refs):
    sources, (out_ref, held, in_sems, out_sems) = refs[:-4], refs[-4:]

    def source(block):
        if not relative:
            return sources[0].at[block // 2, block % 2]
        step, other = block // 4, block // 2 % 2
        return sources[4].at[step, block % 2] if other else sources[step].at[0, block % 2]

    def name(block):
        if not relative:
            return block
        return 2 * band_at(band_ref[0], 4 - block // 4, block // 2 % 2) + block % 2

    def fetch(block):
        return pltpu.make_async_copy(source(block), held.at[block], in_sems.at[block])

    def send(block):
        slot = jnp.maximum(table_ref[name(block)], 0)
        return pltpu.make_async_copy(held.at[block], out_ref.at[slot], out_sems.at[block])

    for block in range(16):
        fetch(block).start()
    for block in range(16):
        fetch(block).wait()

        @pl.when(table_ref[name(block)] >= 0)
        def _():
            send(block).start()

    for block in range(16):

        @pl.when(table_ref[name(block)] >= 0)
        def _():
            send(block).wait()


def pack(table, band, *sources):
    shape, kind = sources[0].shape[2:], sources[0].dtype
    return pl.pallas_call(
        functools.partial(pack_kernel, len(sources) > 1),
        grid_spec=pltpu.PrefetchScalarGridSpec(
            num_scalar_prefetch=2,
            grid=(1,),
            in_specs=[pl.BlockSpec(memory_space=pl.ANY)] * len(sources),
            out_specs=pl.BlockSpec(memory_space=pl.ANY),
            scratch_shapes=[
                pltpu.VMEM((16,) + shape, kind),
                pltpu.SemaphoreType.DMA((16,)),
                pltpu.SemaphoreType.DMA((16,)),
            ],
        ),
        out_shape=jax.ShapeDtypeStruct((32,) + shape, kind),
        compiler_params=pltpu.CompilerParams(vmem_limit_bytes=VMEM_LIMIT),
        name="pack",
    )(table, band, *sources)


def image_kernel(chunks, ids_ref, offsets_ref, *refs):
    arrived = refs[:chunks]
    angle_ref, range_ref, out_ref, total, turned, angle = refs[chunks:]
    step = pl.program_id(0)
    heights = [part.shape[2] for part in arrived]

    @pl.when(step == 0)
    def _():
        angle[...] = jnp.transpose(angle_ref[...].astype(jnp.float32)).astype(jnp.bfloat16)

    @pl.when(step < 4)
    def _():
        total[...] = jnp.zeros_like(total)
        for slot in range(32):
            target = ids_ref[slot]

            @pl.when(target >= 0)
            def _():
                for chunk in range(chunks):
                    rows = pl.ds(sum(heights[:chunk]), heights[chunk])
                    total[target, :, rows, :] += arrived[chunk][slot].astype(jnp.float32)

        for image in range(8):
            both = [total[2 * image : 2 * image + 2, b].reshape(256, 128) for b in range(2)]
            both = jnp.concatenate(both, 1).astype(jnp.bfloat16)
            product = jnp.dot(angle[...], both, preferred_element_type=jnp.float32).astype(jnp.bfloat16)
            for b in range(2):
                rows = pl.ds(256 * image, 256)
                turned[2 * step + b, rows, :] = product[:, 128 * b : 128 * b + 128]

    @pl.when(step >= 4)
    def _():
        start = offsets_ref[jnp.maximum(step - 4, 0)]
        for half in range(2):
            rows = pl.ds(1024 * half, 1024)
            slab = jnp.concatenate([turned[start + i, rows, :] for i in range(3)], 1)
            product = jnp.dot(slab, range_ref[0], preferred_element_type=jnp.float32)
            out_ref[rows, :] = product.astype(jnp.bfloat16)


def form_images(ids, offsets, arrived, angle, range_weights):
    chunks = len(arrived)
    return pl.pallas_call(
        functools.partial(image_kernel, chunks),
        grid_spec=pltpu.PrefetchScalarGridSpec(
            num_scalar_prefetch=2,
            grid=(12,),
            in_specs=[
                pl.BlockSpec((32, 2, part.shape[2], 128), lambda s, *_: (0, jnp.minimum(s, 3), 0, 0))
                for part in arrived
            ]
            + [
                pl.BlockSpec((256, 256), lambda s, *_: (0, 0)),
                pl.BlockSpec((1, 384, 128), lambda s, *_: (jnp.maximum(s - 4, 0), 0, 0)),
            ],
            out_specs=pl.BlockSpec((2048, 128), lambda s, *_: (0, jnp.maximum(s - 4, 0))),
            scratch_shapes=[
                pltpu.VMEM((16, 2, 128, 128), jnp.float32),
                pltpu.VMEM((8, 2048, 128), jnp.bfloat16),
                pltpu.VMEM((256, 256), jnp.bfloat16),
            ],
        ),
        out_shape=jax.ShapeDtypeStruct((2048, 1024), jnp.bfloat16),
        compiler_params=pltpu.CompilerParams(vmem_limit_bytes=VMEM_LIMIT),
        name="form_images",
    )(ids, offsets, *arrived, angle, range_weights)


def angle_matrix(steering, angle_weights):
    both = jnp.einsum("pya,sae->pyse", angle_weights, steering, preferred_element_type=jnp.float32)
    real, imag = both[:, :, 0], both[:, :, 1]
    full = jnp.stack([jnp.stack([real, -imag], 2), jnp.stack([imag, real], 2)], 0)
    full = full.astype(jnp.bfloat16).reshape(2, 2, 128, 2, 8, 8)
    return full.transpose(1, 5, 3, 4, 0, 2).reshape(256, 256)


def routing(merge_owner, merge_slot, ping_index):
    owners = merge_owner.reshape(16, 16)
    slots = merge_slot.reshape(16, 16)
    place = jnp.arange(16, dtype=jnp.int32)
    same = (owners[:, :, None] == owners[:, None, :]) & (place[None, :, None] > place[None, None, :])
    rank = jnp.sum(same.astype(jnp.int32), 2)
    leaving = jnp.where(owners >= 0, owners * 2 + rank, -1)
    table = lax.dynamic_index_in_dim(leaving, ping_index, 0, keepdims=False)
    pair = jnp.arange(2, dtype=jnp.int32)
    coming = (owners[:, None, :] == ping_index) & (rank[:, None, :] == pair[None, :, None])
    target = slots * 2 + place[None, :] % 2
    ids = jnp.sum(jnp.where(coming, target[:, None, :] + 1, 0), 2) - 1
    return table, ids.reshape(32)


def to_owners(some, outgoing):
    def exchange(blocks):
        return lax.all_to_all(blocks, "ping", split_axis=0, concat_axis=0, tiled=True)

    return lax.cond(some, exchange, lambda blocks: blocks, outgoing)


def flat(part):
    return part.reshape(part.shape[:3] + (-1, 128))


def ring_step(step, other):
    return [(band, ((band // 2 + step) % 4) * 2 + (band + other) % 2) for band in range(8)]


def on_device(echoes, replica, steering, angle_weights, range_weights, range_offsets, merge_owner, merge_slot):
    ping_index = lax.axis_index("ping")
    x = echoes.reshape(16, 8, 2, 64, 128).transpose(0, 1, 3, 2, 4).reshape(16, 8, 128, 128)
    table, ids = routing(merge_owner, merge_slot, ping_index)
    angle = angle_matrix(steering, angle_weights)
    band_index = lax.axis_index("band")
    band = band_index.reshape(1).astype(jnp.int32)
    (sent,) = compress(band, x, replica, 0, SPLIT, False)
    band_tile = lax.all_to_all(sent, "band", split_axis=0, concat_axis=0, tiled=True)
    ring = compress(band, x, replica, SPLIT, 8 - SPLIT, True)
    outgoing = pack(table, band, flat(band_tile))
    some = jnp.any(merge_owner >= 0)
    outgoing, ids, angle, some, *ring = lax.optimization_barrier((outgoing, ids, angle, some, *ring))
    moved = [ring[0]] + [lax.ppermute(ring[step], "band", ring_step(step, 0)) for step in (1, 2, 3)]
    first = to_owners(some, outgoing)
    first, *moved = lax.optimization_barrier((first, *moved))
    others = lax.ppermute(jnp.stack([part[1] for part in moved]), "band", ring_step(0, 1))
    outgoing = pack(table, band, *[flat(part) for part in moved], flat(others))
    second = lax.all_to_all(outgoing, "ping", split_axis=0, concat_axis=0, tiled=True)
    arrived = [first, second]
    merged = form_images(ids, range_offsets, arrived, angle, range_weights)
    return merged.reshape(8, 2, 128, 1024)


def solution(mesh):
    placed = (
        P(("ping", "band"), None, None, None),
        P(),
        P(),
        P(),
        P("band", None, None),
        P("band"),
        P(),
        P(),
    )
    return jax.shard_map(
        on_device,
        mesh=mesh,
        in_specs=placed,
        out_specs=P("ping", None, None, "band"),
        check_vma=False,
    )
```

```python
import functools

import jax
import jax.numpy as jnp
from jax import lax
from jax.experimental import pallas as pl
from jax.experimental.pallas import tpu as pltpu
from jax.sharding import PartitionSpec as P

SPLIT = 3
VMEM_LIMIT = 56 * 1024 * 1024


def compress_kernel(relative, band_ref, x_ref, taps_ref, *refs):
    row = lax.broadcasted_iota(jnp.int32, (128, 128), 0)
    col = lax.broadcasted_iota(jnp.int32, (128, 128), 1)
    lower, upper = [], []
    for part in range(2):
        line = jnp.broadcast_to(taps_ref[0, part : part + 1, :].astype(jnp.float32), (128, 128))
        circulant = jnp.transpose(pltpu.roll(line, 0, 1, stride=1, stride_axis=0))
        lower.append(jnp.where(row >= col, circulant, 0.0))
        upper.append(jnp.where(row < col, circulant, 0.0))
    weights = jnp.concatenate(
        [
            jnp.concatenate([lower[0], -lower[1]], 1),
            jnp.concatenate([lower[1], lower[0]], 1),
            jnp.concatenate([upper[0], -upper[1]], 1),
            jnp.concatenate([upper[1], upper[0]], 1),
        ],
        0,
    ).astype(jnp.bfloat16)
    wanted = (row & 7) * 16 + ((row >> 3) & 7) * 2 + (row >> 6)
    permute = (wanted == col).astype(jnp.float32).astype(jnp.bfloat16)
    for block in range(2):
        real, imag = [], []
        for tile in range(8):
            rows = x_ref[8 * block : 8 * block + 8, 0, 16 * tile : 16 * tile + 16, :]
            moved = jnp.dot(permute, rows.reshape(128, 128), preferred_element_type=jnp.float32)
            real.append(moved[:64])
            imag.append(moved[64:])
        real = jnp.concatenate(real, 0)
        imag = jnp.concatenate(imag, 0)
        nothing = jnp.zeros((8, 128), jnp.float32)
        real_next = jnp.concatenate([real[8:], nothing], 0)
        imag_next = jnp.concatenate([imag[8:], nothing], 0)
        stacked = jnp.concatenate([real, imag, real_next, imag_next], 1).astype(jnp.bfloat16)
        product = jnp.dot(stacked, weights, preferred_element_type=jnp.float32)
        product = product.reshape(64, 8, 256)
        product = jnp.concatenate([product[:, :, :128], product[:, :, 128:]], 1)
        product = product.astype(jnp.bfloat16).reshape(8, 8, 16, 128)
        if not relative:
            refs[0][:, block, :, 0] = product
            continue
        held = refs[2]
        held[...] = product
        for step in range(4):
            for other in range(2):
                refs[other][step, block, :, 0] = held[band_at(band_ref[0], step, other)]


def band_at(band, step, other):
    return ((band >> 1) + step) % 4 * 2 + ((band & 1) + other) % 2


def compress(band, x, taps, first, count, relative):
    lead, outs = (4, 2) if relative else (8, 1)
    return pl.pallas_call(
        functools.partial(compress_kernel, relative),
        grid_spec=pltpu.PrefetchScalarGridSpec(
            num_scalar_prefetch=1,
            grid=(count,),
            in_specs=[
                pl.BlockSpec((16, 1, 128, 128), lambda i, *_: (0, first + i, 0, 0)),
                pl.BlockSpec((1, 2, 128), lambda i, *_: (first + i, 0, 0)),
            ],
            out_specs=[pl.BlockSpec((lead, 2, 8, 1, 16, 128), lambda i, *_: (0, 0, 0, i, 0, 0))] * outs,
            scratch_shapes=[pltpu.VMEM((8, 8, 16, 128), jnp.bfloat16)] * relative,
        ),
        out_shape=[jax.ShapeDtypeStruct((lead, 2, 8, count, 16, 128), jnp.bfloat16)] * outs,
        compiler_params=pltpu.CompilerParams(vmem_limit_bytes=VMEM_LIMIT),
        name="compress_relative" if relative else "compress",
    )(band, x, taps)


def pack_kernel(relative, table_ref, band_ref, *refs):
    sources, (out_ref, held, in_sems, out_sems) = refs[:-4], refs[-4:]

    def source(block):
        if not relative:
            return sources[0].at[block // 2, block % 2]
        step, other = block // 4, block // 2 % 2
        return sources[step + 1].at[other, block % 2] if step else sources[other].at[0, block % 2]

    def name(block):
        if not relative:
            return block
        return 2 * band_at(band_ref[0], 4 - block // 4, block // 2 % 2) + block % 2

    def fetch(block):
        return pltpu.make_async_copy(source(block), held.at[block], in_sems.at[block])

    def send(block):
        slot = jnp.maximum(table_ref[name(block)], 0)
        return pltpu.make_async_copy(held.at[block], out_ref.at[slot], out_sems.at[block])

    for block in range(16):
        fetch(block).start()
    for block in range(16):
        fetch(block).wait()

        @pl.when(table_ref[name(block)] >= 0)
        def _():
            send(block).start()

    for block in range(16):

        @pl.when(table_ref[name(block)] >= 0)
        def _():
            send(block).wait()


def pack(table, band, *sources):
    shape, kind = sources[0].shape[2:], sources[0].dtype
    return pl.pallas_call(
        functools.partial(pack_kernel, len(sources) > 1),
        grid_spec=pltpu.PrefetchScalarGridSpec(
            num_scalar_prefetch=2,
            grid=(1,),
            in_specs=[pl.BlockSpec(memory_space=pl.ANY)] * len(sources),
            out_specs=pl.BlockSpec(memory_space=pl.ANY),
            scratch_shapes=[
                pltpu.VMEM((16,) + shape, kind),
                pltpu.SemaphoreType.DMA((16,)),
                pltpu.SemaphoreType.DMA((16,)),
            ],
        ),
        out_shape=jax.ShapeDtypeStruct((32,) + shape, kind),
        compiler_params=pltpu.CompilerParams(vmem_limit_bytes=VMEM_LIMIT),
        name="pack",
    )(table, band, *sources)


def image_kernel(chunks, ids_ref, offsets_ref, *refs):
    arrived = refs[:chunks]
    angle_ref, range_ref, out_ref, total, turned, angle = refs[chunks:]
    step = pl.program_id(0)
    heights = [part.shape[2] for part in arrived]

    @pl.when(step == 0)
    def _():
        angle[...] = jnp.transpose(angle_ref[...].astype(jnp.float32)).astype(jnp.bfloat16)

    @pl.when(step < 4)
    def _():
        total[...] = jnp.zeros_like(total)
        for slot in range(32):
            target = ids_ref[slot]

            @pl.when(target >= 0)
            def _():
                for chunk in range(chunks):
                    rows = pl.ds(sum(heights[:chunk]), heights[chunk])
                    total[target, :, rows, :] += arrived[chunk][slot].astype(jnp.float32)

        for image in range(8):
            both = [total[2 * image : 2 * image + 2, b].reshape(256, 128) for b in range(2)]
            both = jnp.concatenate(both, 1).astype(jnp.bfloat16)
            product = jnp.dot(angle[...], both, preferred_element_type=jnp.float32).astype(jnp.bfloat16)
            for b in range(2):
                rows = pl.ds(256 * image, 256)
                turned[2 * step + b, rows, :] = product[:, 128 * b : 128 * b + 128]

    @pl.when(step >= 4)
    def _():
        start = offsets_ref[jnp.maximum(step - 4, 0)]
        for half in range(2):
            rows = pl.ds(1024 * half, 1024)
            slab = jnp.concatenate([turned[start + i, rows, :] for i in range(3)], 1)
            product = jnp.dot(slab, range_ref[0], preferred_element_type=jnp.float32)
            out_ref[rows, :] = product.astype(jnp.bfloat16)


def form_images(ids, offsets, arrived, angle, range_weights):
    chunks = len(arrived)
    return pl.pallas_call(
        functools.partial(image_kernel, chunks),
        grid_spec=pltpu.PrefetchScalarGridSpec(
            num_scalar_prefetch=2,
            grid=(12,),
            in_specs=[
                pl.BlockSpec((32, 2, part.shape[2], 128), lambda s, *_: (0, jnp.minimum(s, 3), 0, 0))
                for part in arrived
            ]
            + [
                pl.BlockSpec((256, 256), lambda s, *_: (0, 0)),
                pl.BlockSpec((1, 384, 128), lambda s, *_: (jnp.maximum(s - 4, 0), 0, 0)),
            ],
            out_specs=pl.BlockSpec((2048, 128), lambda s, *_: (0, jnp.maximum(s - 4, 0))),
            scratch_shapes=[
                pltpu.VMEM((16, 2, 128, 128), jnp.float32),
                pltpu.VMEM((8, 2048, 128), jnp.bfloat16),
                pltpu.VMEM((256, 256), jnp.bfloat16),
            ],
        ),
        out_shape=jax.ShapeDtypeStruct((2048, 1024), jnp.bfloat16),
        compiler_params=pltpu.CompilerParams(vmem_limit_bytes=VMEM_LIMIT),
        name="form_images",
    )(ids, offsets, *arrived, angle, range_weights)


def angle_matrix(steering, angle_weights):
    both = jnp.einsum("pya,sae->pyse", angle_weights, steering, preferred_element_type=jnp.float32)
    real, imag = both[:, :, 0], both[:, :, 1]
    full = jnp.stack([jnp.stack([real, -imag], 2), jnp.stack([imag, real], 2)], 0)
    full = full.astype(jnp.bfloat16).reshape(2, 2, 128, 2, 8, 8)
    return full.transpose(1, 5, 3, 4, 0, 2).reshape(256, 256)


def routing(merge_owner, merge_slot, ping_index):
    owners = merge_owner.reshape(16, 16)
    slots = merge_slot.reshape(16, 16)
    place = jnp.arange(16, dtype=jnp.int32)
    same = (owners[:, :, None] == owners[:, None, :]) & (place[None, :, None] > place[None, None, :])
    rank = jnp.sum(same.astype(jnp.int32), 2)
    leaving = jnp.where(owners >= 0, owners * 2 + rank, -1)
    table = lax.dynamic_index_in_dim(leaving, ping_index, 0, keepdims=False)
    pair = jnp.arange(2, dtype=jnp.int32)
    coming = (owners[:, None, :] == ping_index) & (rank[:, None, :] == pair[None, :, None])
    target = slots * 2 + place[None, :] % 2
    ids = jnp.sum(jnp.where(coming, target[:, None, :] + 1, 0), 2) - 1
    return table, ids.reshape(32)


def to_owners(some, outgoing):
    def exchange(blocks):
        return lax.all_to_all(blocks, "ping", split_axis=0, concat_axis=0, tiled=True)

    return lax.cond(some, exchange, lambda blocks: blocks, outgoing)


def flat(part):
    return part.reshape(part.shape[:3] + (-1, 128))


def ring_step(step, other):
    return [(band, ((band // 2 + step) % 4) * 2 + (band + other) % 2) for band in range(8)]


def on_device(echoes, replica, steering, angle_weights, range_weights, range_offsets, merge_owner, merge_slot):
    ping_index = lax.axis_index("ping")
    x = echoes.reshape(16, 8, 2, 64, 128).transpose(0, 1, 3, 2, 4).reshape(16, 8, 128, 128)
    table, ids = routing(merge_owner, merge_slot, ping_index)
    angle = angle_matrix(steering, angle_weights)
    band_index = lax.axis_index("band")
    band = band_index.reshape(1).astype(jnp.int32)
    (sent,) = compress(band, x, replica, 0, SPLIT, False)
    band_tile = lax.all_to_all(sent, "band", split_axis=0, concat_axis=0, tiled=True)
    same, other = compress(band, x, replica, SPLIT, 8 - SPLIT, True)
    other = lax.ppermute(other, "band", ring_step(0, 1))
    ring = [jnp.stack([same[step], other[step]]) for step in (1, 2, 3)]
    outgoing = pack(table, band, flat(band_tile))
    some = jnp.any(merge_owner >= 0)
    outgoing, ids, angle, some, same, other, *ring = lax.optimization_barrier(
        (outgoing, ids, angle, some, same, other, *ring)
    )
    ring = [lax.ppermute(part, "band", ring_step(step + 1, 0)) for step, part in enumerate(ring)]
    first = to_owners(some, outgoing)
    first, *ring = lax.optimization_barrier((first, *ring))
    outgoing = pack(table, band, *[flat(part) for part in (same, other, *ring)])
    second = lax.all_to_all(outgoing, "ping", split_axis=0, concat_axis=0, tiled=True)
    arrived = [first, second]
    merged = form_images(ids, range_offsets, arrived, angle, range_weights)
    return merged.reshape(8, 2, 128, 1024)


def solution(mesh):
    placed = (
        P(("ping", "band"), None, None, None),
        P(),
        P(),
        P(),
        P("band", None, None),
        P("band"),
        P(),
        P(),
    )
    return jax.shard_map(
        on_device,
        mesh=mesh,
        in_specs=placed,
        out_specs=P("ping", None, None, "band"),
        check_vma=False,
    )
```

```python
import functools

import jax
import jax.numpy as jnp
from jax import lax
from jax.experimental import pallas as pl
from jax.experimental.pallas import tpu as pltpu
from jax.sharding import PartitionSpec as P

SPLIT = 3
VMEM_LIMIT = 56 * 1024 * 1024


def compress_kernel(relative, band_ref, x_ref, taps_ref, *refs):
    row = lax.broadcasted_iota(jnp.int32, (128, 128), 0)
    col = lax.broadcasted_iota(jnp.int32, (128, 128), 1)
    lower, upper = [], []
    for part in range(2):
        line = jnp.broadcast_to(taps_ref[0, part : part + 1, :].astype(jnp.float32), (128, 128))
        circulant = jnp.transpose(pltpu.roll(line, 0, 1, stride=1, stride_axis=0))
        lower.append(jnp.where(row >= col, circulant, 0.0))
        upper.append(jnp.where(row < col, circulant, 0.0))
    weights = jnp.concatenate(
        [
            jnp.concatenate([lower[0], -lower[1]], 1),
            jnp.concatenate([lower[1], lower[0]], 1),
            jnp.concatenate([upper[0], -upper[1]], 1),
            jnp.concatenate([upper[1], upper[0]], 1),
        ],
        0,
    ).astype(jnp.bfloat16)
    wanted = (row & 7) * 16 + ((row >> 3) & 7) * 2 + (row >> 6)
    permute = (wanted == col).astype(jnp.float32).astype(jnp.bfloat16)
    for block in range(2):
        real, imag = [], []
        for tile in range(8):
            rows = x_ref[8 * block : 8 * block + 8, 0, 16 * tile : 16 * tile + 16, :]
            moved = jnp.dot(permute, rows.reshape(128, 128), preferred_element_type=jnp.float32)
            real.append(moved[:64])
            imag.append(moved[64:])
        real = jnp.concatenate(real, 0)
        imag = jnp.concatenate(imag, 0)
        nothing = jnp.zeros((8, 128), jnp.float32)
        real_next = jnp.concatenate([real[8:], nothing], 0)
        imag_next = jnp.concatenate([imag[8:], nothing], 0)
        stacked = jnp.concatenate([real, imag, real_next, imag_next], 1).astype(jnp.bfloat16)
        product = jnp.dot(stacked, weights, preferred_element_type=jnp.float32)
        product = product.reshape(64, 8, 256)
        product = jnp.concatenate([product[:, :, :128], product[:, :, 128:]], 1)
        product = product.astype(jnp.bfloat16).reshape(8, 8, 16, 128)
        if not relative:
            refs[0][:, block, :, 0] = product
            continue
        held = refs[2]
        held[...] = product
        for step in range(4):
            for other in range(2):
                refs[other][step, block, :, 0] = held[band_at(band_ref[0], step, other)]


def band_at(band, step, other):
    return ((band >> 1) + step) % 4 * 2 + ((band & 1) + other) % 2


def compress(band, x, taps, first, count, relative):
    lead, outs = (4, 2) if relative else (8, 1)
    return pl.pallas_call(
        functools.partial(compress_kernel, relative),
        grid_spec=pltpu.PrefetchScalarGridSpec(
            num_scalar_prefetch=1,
            grid=(count,),
            in_specs=[
                pl.BlockSpec((16, 1, 128, 128), lambda i, *_: (0, first + i, 0, 0)),
                pl.BlockSpec((1, 2, 128), lambda i, *_: (first + i, 0, 0)),
            ],
            out_specs=[pl.BlockSpec((lead, 2, 8, 1, 16, 128), lambda i, *_: (0, 0, 0, i, 0, 0))] * outs,
            scratch_shapes=[pltpu.VMEM((8, 8, 16, 128), jnp.bfloat16)] * relative,
        ),
        out_shape=[jax.ShapeDtypeStruct((lead, 2, 8, count, 16, 128), jnp.bfloat16)] * outs,
        compiler_params=pltpu.CompilerParams(vmem_limit_bytes=VMEM_LIMIT),
        name="compress_relative" if relative else "compress",
    )(band, x, taps)


def pack_kernel(relative, table_ref, band_ref, *refs):
    sources, (out_ref, sems) = refs[:-2], refs[-2:]

    def source(block):
        if not relative:
            return sources[0].at[block // 2, block % 2]
        step, other = block // 4, block // 2 % 2
        return sources[step + 1].at[other, block % 2] if step else sources[other].at[0, block % 2]

    def name(block):
        if not relative:
            return block
        return 2 * band_at(band_ref[0], 4 - block // 4, block // 2 % 2) + block % 2

    def send(block):
        slot = jnp.maximum(table_ref[name(block)], 0)
        return pltpu.make_async_copy(source(block), out_ref.at[slot], sems.at[block])

    for block in range(16):

        @pl.when(table_ref[name(block)] >= 0)
        def _():
            send(block).start()

    for block in range(16):

        @pl.when(table_ref[name(block)] >= 0)
        def _():
            send(block).wait()


def pack(table, band, *sources):
    shape, kind = sources[0].shape[2:], sources[0].dtype
    sources = [pltpu.with_memory_space_constraint(source, pltpu.VMEM) for source in sources]
    return pl.pallas_call(
        functools.partial(pack_kernel, len(sources) > 1),
        grid_spec=pltpu.PrefetchScalarGridSpec(
            num_scalar_prefetch=2,
            grid=(1,),
            in_specs=[pl.BlockSpec(memory_space=pltpu.VMEM)] * len(sources),
            out_specs=pl.BlockSpec(memory_space=pl.ANY),
            scratch_shapes=[pltpu.SemaphoreType.DMA((16,))],
        ),
        out_shape=jax.ShapeDtypeStruct((32,) + shape, kind),
        compiler_params=pltpu.CompilerParams(vmem_limit_bytes=VMEM_LIMIT),
        name="pack",
    )(table, band, *sources)


def image_kernel(chunks, ids_ref, offsets_ref, *refs):
    arrived = refs[:chunks]
    angle_ref, range_ref, out_ref, total, turned, angle = refs[chunks:]
    step = pl.program_id(0)
    heights = [part.shape[2] for part in arrived]

    @pl.when(step == 0)
    def _():
        angle[...] = jnp.transpose(angle_ref[...].astype(jnp.float32)).astype(jnp.bfloat16)

    @pl.when(step < 4)
    def _():
        total[...] = jnp.zeros_like(total)
        for slot in range(32):
            target = ids_ref[slot]

            @pl.when(target >= 0)
            def _():
                for chunk in range(chunks):
                    rows = pl.ds(sum(heights[:chunk]), heights[chunk])
                    total[target, :, rows, :] += arrived[chunk][slot].astype(jnp.float32)

        for image in range(8):
            both = [total[2 * image : 2 * image + 2, b].reshape(256, 128) for b in range(2)]
            both = jnp.concatenate(both, 1).astype(jnp.bfloat16)
            product = jnp.dot(angle[...], both, preferred_element_type=jnp.float32).astype(jnp.bfloat16)
            for b in range(2):
                rows = pl.ds(256 * image, 256)
                turned[2 * step + b, rows, :] = product[:, 128 * b : 128 * b + 128]

    @pl.when(step >= 4)
    def _():
        for one in range(2):
            start = offsets_ref[jnp.maximum(step - 4, 0) * 2 + one]
            columns = pl.ds(128 * one, 128)
            for half in range(2):
                rows = pl.ds(1024 * half, 1024)
                slab = jnp.concatenate([turned[start + i, rows, :] for i in range(3)], 1)
                product = jnp.dot(slab, range_ref[one], preferred_element_type=jnp.float32)
                out_ref[rows, columns] = product.astype(jnp.bfloat16)


def form_images(ids, offsets, arrived, angle, range_weights):
    chunks = len(arrived)
    return pl.pallas_call(
        functools.partial(image_kernel, chunks),
        grid_spec=pltpu.PrefetchScalarGridSpec(
            num_scalar_prefetch=2,
            grid=(8,),
            in_specs=[
                pl.BlockSpec((32, 2, part.shape[2], 128), lambda s, *_: (0, jnp.minimum(s, 3), 0, 0))
                for part in arrived
            ]
            + [
                pl.BlockSpec((256, 256), lambda s, *_: (0, 0)),
                pl.BlockSpec((2, 384, 128), lambda s, *_: (jnp.maximum(s - 4, 0), 0, 0)),
            ],
            out_specs=pl.BlockSpec((2048, 256), lambda s, *_: (0, jnp.maximum(s - 4, 0))),
            scratch_shapes=[
                pltpu.VMEM((16, 2, 128, 128), jnp.float32),
                pltpu.VMEM((8, 2048, 128), jnp.bfloat16),
                pltpu.VMEM((256, 256), jnp.bfloat16),
            ],
        ),
        out_shape=jax.ShapeDtypeStruct((2048, 1024), jnp.bfloat16),
        compiler_params=pltpu.CompilerParams(vmem_limit_bytes=VMEM_LIMIT),
        name="form_images",
    )(ids, offsets, *arrived, angle, range_weights)


def angle_matrix(steering, angle_weights):
    both = jnp.einsum("pya,sae->pyse", angle_weights, steering, preferred_element_type=jnp.float32)
    real, imag = both[:, :, 0], both[:, :, 1]
    full = jnp.stack([jnp.stack([real, -imag], 2), jnp.stack([imag, real], 2)], 0)
    full = full.astype(jnp.bfloat16).reshape(2, 2, 128, 2, 8, 8)
    return full.transpose(1, 5, 3, 4, 0, 2).reshape(256, 256)


def routing(merge_owner, merge_slot, ping_index):
    owners = merge_owner.reshape(16, 16)
    slots = merge_slot.reshape(16, 16)
    place = jnp.arange(16, dtype=jnp.int32)
    same = (owners[:, :, None] == owners[:, None, :]) & (place[None, :, None] > place[None, None, :])
    rank = jnp.sum(same.astype(jnp.int32), 2)
    leaving = jnp.where(owners >= 0, owners * 2 + rank, -1)
    table = lax.dynamic_index_in_dim(leaving, ping_index, 0, keepdims=False)
    pair = jnp.arange(2, dtype=jnp.int32)
    coming = (owners[:, None, :] == ping_index) & (rank[:, None, :] == pair[None, :, None])
    target = slots * 2 + place[None, :] % 2
    ids = jnp.sum(jnp.where(coming, target[:, None, :] + 1, 0), 2) - 1
    return table, ids.reshape(32)


def to_owners(some, outgoing):
    def exchange(blocks):
        return lax.all_to_all(blocks, "ping", split_axis=0, concat_axis=0, tiled=True)

    return lax.cond(some, exchange, lambda blocks: blocks, outgoing)


def flat(part):
    return part.reshape(part.shape[:3] + (-1, 128))


def ring_step(step, other):
    return [(band, ((band // 2 + step) % 4) * 2 + (band + other) % 2) for band in range(8)]


def on_device(echoes, replica, steering, angle_weights, range_weights, range_offsets, merge_owner, merge_slot):
    ping_index = lax.axis_index("ping")
    x = echoes.reshape(16, 8, 2, 64, 128).transpose(0, 1, 3, 2, 4).reshape(16, 8, 128, 128)
    table, ids = routing(merge_owner, merge_slot, ping_index)
    angle = angle_matrix(steering, angle_weights)
    band_index = lax.axis_index("band")
    band = band_index.reshape(1).astype(jnp.int32)
    (sent,) = compress(band, x, replica, 0, SPLIT, False)
    band_tile = lax.all_to_all(sent, "band", split_axis=0, concat_axis=0, tiled=True)
    same, other = compress(band, x, replica, SPLIT, 8 - SPLIT, True)
    other = lax.ppermute(other, "band", ring_step(0, 1))
    ring = [jnp.stack([same[step], other[step]]) for step in (1, 2, 3)]
    outgoing = pack(table, band, flat(band_tile))
    some = jnp.any(merge_owner >= 0)
    outgoing, ids, angle, some, same, other, *ring = lax.optimization_barrier(
        (outgoing, ids, angle, some, same, other, *ring)
    )
    ring = [lax.ppermute(part, "band", ring_step(step + 1, 0)) for step, part in enumerate(ring)]
    first = to_owners(some, outgoing)
    first, *ring = lax.optimization_barrier((first, *ring))
    outgoing = pack(table, band, *[flat(part) for part in (same, other, *ring)])
    second = lax.all_to_all(outgoing, "ping", split_axis=0, concat_axis=0, tiled=True)
    arrived = [first, second]
    merged = form_images(ids, range_offsets, arrived, angle, range_weights)
    return merged.reshape(8, 2, 128, 1024)


def solution(mesh):
    placed = (
        P(("ping", "band"), None, None, None),
        P(),
        P(),
        P(),
        P("band", None, None),
        P("band"),
        P(),
        P(),
    )
    return jax.shard_map(
        on_device,
        mesh=mesh,
        in_specs=placed,
        out_specs=P("ping", None, None, "band"),
        check_vma=False,
    )
```

```python
import functools

import jax
import jax.numpy as jnp
from jax import lax
from jax.experimental import pallas as pl
from jax.experimental.pallas import tpu as pltpu
from jax.sharding import PartitionSpec as P

SPLIT = 3
VMEM_LIMIT = 56 * 1024 * 1024


def compress_kernel(relative, band_ref, x_ref, taps_ref, *refs):
    row = lax.broadcasted_iota(jnp.int32, (128, 128), 0)
    col = lax.broadcasted_iota(jnp.int32, (128, 128), 1)
    lower, upper = [], []
    for part in range(2):
        line = jnp.broadcast_to(taps_ref[0, part : part + 1, :].astype(jnp.float32), (128, 128))
        circulant = jnp.transpose(pltpu.roll(line, 0, 1, stride=1, stride_axis=0))
        lower.append(jnp.where(row >= col, circulant, 0.0))
        upper.append(jnp.where(row < col, circulant, 0.0))
    weights = jnp.concatenate(
        [
            jnp.concatenate([lower[0], -lower[1]], 1),
            jnp.concatenate([lower[1], lower[0]], 1),
            jnp.concatenate([upper[0], -upper[1]], 1),
            jnp.concatenate([upper[1], upper[0]], 1),
        ],
        0,
    ).astype(jnp.bfloat16)
    wanted = (row & 7) * 16 + ((row >> 3) & 7) * 2 + (row >> 6)
    permute = (wanted == col).astype(jnp.float32).astype(jnp.bfloat16)
    for block in range(2):
        real, imag = [], []
        for tile in range(8):
            rows = x_ref[8 * block : 8 * block + 8, 0, 16 * tile : 16 * tile + 16, :]
            moved = jnp.dot(permute, rows.reshape(128, 128), preferred_element_type=jnp.float32)
            real.append(moved[:64])
            imag.append(moved[64:])
        real = jnp.concatenate(real, 0)
        imag = jnp.concatenate(imag, 0)
        nothing = jnp.zeros((8, 128), jnp.float32)
        real_next = jnp.concatenate([real[8:], nothing], 0)
        imag_next = jnp.concatenate([imag[8:], nothing], 0)
        stacked = jnp.concatenate([real, imag, real_next, imag_next], 1).astype(jnp.bfloat16)
        product = jnp.dot(stacked, weights, preferred_element_type=jnp.float32)
        product = product.reshape(64, 8, 256)
        product = jnp.concatenate([product[:, :, :128], product[:, :, 128:]], 1)
        product = product.astype(jnp.bfloat16).reshape(8, 8, 16, 128)
        if not relative:
            refs[0][:, block, :, 0] = product
            continue
        held = refs[2]
        held[...] = product
        for step in range(4):
            for other in range(2):
                refs[other][step, block, :, 0] = held[band_at(band_ref[0], step, other)]


def band_at(band, step, other):
    return ((band >> 1) + step) % 4 * 2 + ((band & 1) + other) % 2


def compress(band, x, taps, first, count, relative):
    lead, outs = (4, 2) if relative else (8, 1)
    return pl.pallas_call(
        functools.partial(compress_kernel, relative),
        grid_spec=pltpu.PrefetchScalarGridSpec(
            num_scalar_prefetch=1,
            grid=(count,),
            in_specs=[
                pl.BlockSpec((16, 1, 128, 128), lambda i, *_: (0, first + i, 0, 0)),
                pl.BlockSpec((1, 2, 128), lambda i, *_: (first + i, 0, 0)),
            ],
            out_specs=[pl.BlockSpec((lead, 2, 8, 1, 16, 128), lambda i, *_: (0, 0, 0, i, 0, 0))] * outs,
            scratch_shapes=[pltpu.VMEM((8, 8, 16, 128), jnp.bfloat16)] * relative,
        ),
        out_shape=[jax.ShapeDtypeStruct((lead, 2, 8, count, 16, 128), jnp.bfloat16)] * outs,
        compiler_params=pltpu.CompilerParams(vmem_limit_bytes=VMEM_LIMIT),
        name="compress_relative" if relative else "compress",
    )(band, x, taps)


def pack_kernel(relative, table_ref, band_ref, *refs):
    sources, (out_ref, sems) = refs[:-2], refs[-2:]

    def source(block):
        if not relative:
            return sources[0].at[block // 2, block % 2]
        step, other = block // 4, block // 2 % 2
        return sources[step + 1].at[other, block % 2] if step else sources[other].at[0, block % 2]

    def name(block):
        if not relative:
            return block
        return 2 * band_at(band_ref[0], 4 - block // 4, block // 2 % 2) + block % 2

    def send(block):
        slot = jnp.maximum(table_ref[name(block)], 0)
        return pltpu.make_async_copy(source(block), out_ref.at[slot], sems.at[block])

    for block in range(16):

        @pl.when(table_ref[name(block)] >= 0)
        def _():
            send(block).start()

    for block in range(16):

        @pl.when(table_ref[name(block)] >= 0)
        def _():
            send(block).wait()


def pack(table, band, *sources):
    shape, kind = sources[0].shape[2:], sources[0].dtype
    sources = [pltpu.with_memory_space_constraint(source, pltpu.VMEM) for source in sources]
    return pl.pallas_call(
        functools.partial(pack_kernel, len(sources) > 1),
        grid_spec=pltpu.PrefetchScalarGridSpec(
            num_scalar_prefetch=2,
            grid=(1,),
            in_specs=[pl.BlockSpec(memory_space=pltpu.VMEM)] * len(sources),
            out_specs=pl.BlockSpec(memory_space=pl.ANY),
            scratch_shapes=[pltpu.SemaphoreType.DMA((16,))],
        ),
        out_shape=jax.ShapeDtypeStruct((32,) + shape, kind),
        compiler_params=pltpu.CompilerParams(vmem_limit_bytes=VMEM_LIMIT),
        name="pack",
    )(table, band, *sources)


def image_kernel(chunks, ids_ref, offsets_ref, *refs):
    arrived = refs[:chunks]
    angle_ref, range_ref, out_ref, total, turned, angle = refs[chunks:]
    step = pl.program_id(0)
    heights = [part.shape[2] for part in arrived]

    @pl.when(step == 0)
    def _():
        angle[...] = jnp.transpose(angle_ref[...].astype(jnp.float32)).astype(jnp.bfloat16)

    @pl.when(step < 4)
    def _():
        total[...] = jnp.zeros_like(total)
        for slot in range(32):
            target = ids_ref[slot]

            @pl.when(target >= 0)
            def _():
                for chunk in range(chunks):
                    rows = pl.ds(sum(heights[:chunk]), heights[chunk])
                    total[target, :, rows, :] += arrived[chunk][slot].astype(jnp.float32)

        for image in range(8):
            both = [total[2 * image : 2 * image + 2, b].reshape(256, 128) for b in range(2)]
            both = jnp.concatenate(both, 1).astype(jnp.bfloat16)
            product = jnp.dot(angle[...], both, preferred_element_type=jnp.float32).astype(jnp.bfloat16)
            for b in range(2):
                rows = pl.ds(256 * image, 256)
                turned[2 * step + b, rows, :] = product[:, 128 * b : 128 * b + 128]

    @pl.when(step >= 4)
    def _():
        for one in range(2):
            start = offsets_ref[jnp.maximum(step - 4, 0) * 2 + one]
            columns = pl.ds(128 * one, 128)
            for half in range(2):
                rows = pl.ds(1024 * half, 1024)
                slab = jnp.concatenate([turned[start + i, rows, :] for i in range(3)], 1)
                product = jnp.dot(slab, range_ref[one], preferred_element_type=jnp.float32)
                out_ref[rows, columns] = product.astype(jnp.bfloat16)


def form_images(ids, offsets, arrived, angle, range_weights):
    chunks = len(arrived)
    return pl.pallas_call(
        functools.partial(image_kernel, chunks),
        grid_spec=pltpu.PrefetchScalarGridSpec(
            num_scalar_prefetch=2,
            grid=(8,),
            in_specs=[
                pl.BlockSpec((32, 2, part.shape[2], 128), lambda s, *_: (0, jnp.minimum(s, 3), 0, 0))
                for part in arrived
            ]
            + [
                pl.BlockSpec((256, 256), lambda s, *_: (0, 0)),
                pl.BlockSpec((2, 384, 128), lambda s, *_: (jnp.maximum(s - 4, 0), 0, 0)),
            ],
            out_specs=pl.BlockSpec((2048, 256), lambda s, *_: (0, jnp.maximum(s - 4, 0))),
            scratch_shapes=[
                pltpu.VMEM((16, 2, 128, 128), jnp.float32),
                pltpu.VMEM((8, 2048, 128), jnp.bfloat16),
                pltpu.VMEM((256, 256), jnp.bfloat16),
            ],
        ),
        out_shape=jax.ShapeDtypeStruct((2048, 1024), jnp.bfloat16),
        compiler_params=pltpu.CompilerParams(vmem_limit_bytes=VMEM_LIMIT),
        name="form_images",
    )(ids, offsets, *arrived, angle, range_weights)


def angle_matrix(steering, angle_weights):
    both = jnp.einsum("pya,sae->pyse", angle_weights, steering, preferred_element_type=jnp.float32)
    real, imag = both[:, :, 0], both[:, :, 1]
    full = jnp.stack([jnp.stack([real, -imag], 2), jnp.stack([imag, real], 2)], 0)
    full = full.astype(jnp.bfloat16).reshape(2, 2, 128, 2, 8, 8)
    return full.transpose(1, 5, 3, 4, 0, 2).reshape(256, 256)


def routing(merge_owner, merge_slot, ping_index):
    owners = merge_owner.reshape(16, 16)
    slots = merge_slot.reshape(16, 16)
    place = jnp.arange(16, dtype=jnp.int32)
    same = (owners[:, :, None] == owners[:, None, :]) & (place[None, :, None] > place[None, None, :])
    rank = jnp.sum(same.astype(jnp.int32), 2)
    leaving = jnp.where(owners >= 0, owners * 2 + rank, -1)
    table = lax.dynamic_index_in_dim(leaving, ping_index, 0, keepdims=False)
    pair = jnp.arange(2, dtype=jnp.int32)
    coming = (owners[:, None, :] == ping_index) & (rank[:, None, :] == pair[None, :, None])
    target = slots * 2 + place[None, :] % 2
    ids = jnp.sum(jnp.where(coming, target[:, None, :] + 1, 0), 2) - 1
    return table, ids.reshape(32)


def to_owners(some, table, band, source):
    def exchange(table, band, source):
        return lax.all_to_all(pack(table, band, source), "ping", split_axis=0, concat_axis=0, tiled=True)

    def nothing(table, band, source):
        return jnp.zeros((32,) + source.shape[2:], source.dtype)

    return lax.cond(some, exchange, nothing, table, band, source)


def flat(part):
    return part.reshape(part.shape[:3] + (-1, 128))


def ring_step(step, other):
    return [(band, ((band // 2 + step) % 4) * 2 + (band + other) % 2) for band in range(8)]


def on_device(echoes, replica, steering, angle_weights, range_weights, range_offsets, merge_owner, merge_slot):
    ping_index = lax.axis_index("ping")
    x = echoes.reshape(16, 8, 2, 64, 128).transpose(0, 1, 3, 2, 4).reshape(16, 8, 128, 128)
    table, ids = routing(merge_owner, merge_slot, ping_index)
    angle = angle_matrix(steering, angle_weights)
    band_index = lax.axis_index("band")
    band = band_index.reshape(1).astype(jnp.int32)
    (sent,) = compress(band, x, replica, 0, SPLIT, False)
    band_tile = lax.all_to_all(sent, "band", split_axis=0, concat_axis=0, tiled=True)
    same, other = compress(band, x, replica, SPLIT, 8 - SPLIT, True)
    other = lax.ppermute(other, "band", ring_step(0, 1))
    ring = [jnp.stack([same[step], other[step]]) for step in (1, 2, 3)]
    some = jnp.any(merge_owner >= 0)
    band_tile, table, ids, angle, some, same, other, *ring = lax.optimization_barrier(
        (band_tile, table, ids, angle, some, same, other, *ring)
    )
    ring = [lax.ppermute(part, "band", ring_step(step + 1, 0)) for step, part in enumerate(ring)]
    first = to_owners(some, table, band, flat(band_tile))
    first, *ring = lax.optimization_barrier((first, *ring))
    outgoing = pack(table, band, *[flat(part) for part in (same, other, *ring)])
    second = lax.all_to_all(outgoing, "ping", split_axis=0, concat_axis=0, tiled=True)
    arrived = [first, second]
    merged = form_images(ids, range_offsets, arrived, angle, range_weights)
    return merged.reshape(8, 2, 128, 1024)


def solution(mesh):
    placed = (
        P(("ping", "band"), None, None, None),
        P(),
        P(),
        P(),
        P("band", None, None),
        P("band"),
        P(),
        P(),
    )
    return jax.shard_map(
        on_device,
        mesh=mesh,
        in_specs=placed,
        out_specs=P("ping", None, None, "band"),
        check_vma=False,
    )
```

```python
import functools

import jax
import jax.numpy as jnp
from jax import lax
from jax.experimental import pallas as pl
from jax.experimental.pallas import tpu as pltpu
from jax.sharding import PartitionSpec as P

SPLIT = 3
VMEM_LIMIT = 56 * 1024 * 1024


def compress_kernel(relative, band_ref, x_ref, taps_ref, *refs):
    row = lax.broadcasted_iota(jnp.int32, (128, 128), 0)
    col = lax.broadcasted_iota(jnp.int32, (128, 128), 1)
    lower, upper = [], []
    for part in range(2):
        line = jnp.broadcast_to(taps_ref[0, part : part + 1, :].astype(jnp.float32), (128, 128))
        circulant = jnp.transpose(pltpu.roll(line, 0, 1, stride=1, stride_axis=0))
        lower.append(jnp.where(row >= col, circulant, 0.0))
        upper.append(jnp.where(row < col, circulant, 0.0))
    weights = jnp.concatenate(
        [
            jnp.concatenate([lower[0], -lower[1]], 1),
            jnp.concatenate([lower[1], lower[0]], 1),
            jnp.concatenate([upper[0], -upper[1]], 1),
            jnp.concatenate([upper[1], upper[0]], 1),
        ],
        0,
    ).astype(jnp.bfloat16)
    wanted = (row & 7) * 16 + ((row >> 3) & 7) * 2 + (row >> 6)
    permute = (wanted == col).astype(jnp.float32).astype(jnp.bfloat16)
    for block in range(2):
        real, imag = [], []
        for tile in range(8):
            rows = x_ref[8 * block : 8 * block + 8, 0, 16 * tile : 16 * tile + 16, :]
            moved = jnp.dot(permute, rows.reshape(128, 128), preferred_element_type=jnp.float32)
            real.append(moved[:64])
            imag.append(moved[64:])
        real = jnp.concatenate(real, 0)
        imag = jnp.concatenate(imag, 0)
        nothing = jnp.zeros((8, 128), jnp.float32)
        real_next = jnp.concatenate([real[8:], nothing], 0)
        imag_next = jnp.concatenate([imag[8:], nothing], 0)
        stacked = jnp.concatenate([real, imag, real_next, imag_next], 1).astype(jnp.bfloat16)
        product = jnp.dot(stacked, weights, preferred_element_type=jnp.float32)
        product = product.reshape(64, 8, 256)
        product = jnp.concatenate([product[:, :, :128], product[:, :, 128:]], 1)
        product = product.astype(jnp.bfloat16).reshape(8, 8, 16, 128)
        if not relative:
            refs[0][:, block, :, 0] = product
            continue
        held = refs[2]
        held[...] = product
        for step in range(4):
            for other in range(2):
                refs[other][step, block, :, 0] = held[band_at(band_ref[0], step, other)]


def band_at(band, step, other):
    return ((band >> 1) + step) % 4 * 2 + ((band & 1) + other) % 2


def compress(band, x, taps, first, count, relative):
    lead, outs = (4, 2) if relative else (8, 1)
    return pl.pallas_call(
        functools.partial(compress_kernel, relative),
        grid_spec=pltpu.PrefetchScalarGridSpec(
            num_scalar_prefetch=1,
            grid=(count,),
            in_specs=[
                pl.BlockSpec((16, 1, 128, 128), lambda i, *_: (0, first + i, 0, 0)),
                pl.BlockSpec((1, 2, 128), lambda i, *_: (first + i, 0, 0)),
            ],
            out_specs=[pl.BlockSpec((lead, 2, 8, 1, 16, 128), lambda i, *_: (0, 0, 0, i, 0, 0))] * outs,
            scratch_shapes=[pltpu.VMEM((8, 8, 16, 128), jnp.bfloat16)] * relative,
        ),
        out_shape=[jax.ShapeDtypeStruct((lead, 2, 8, count, 16, 128), jnp.bfloat16)] * outs,
        compiler_params=pltpu.CompilerParams(vmem_limit_bytes=VMEM_LIMIT),
        name="compress_relative" if relative else "compress",
    )(band, x, taps)


def pack_kernel(relative, table_ref, band_ref, *refs):
    sources, (out_ref, sems) = refs[:-2], refs[-2:]

    def source(block):
        if not relative:
            return sources[0].at[block // 2, block % 2]
        step, other = block // 4, block // 2 % 2
        return sources[step + 1].at[other, block % 2] if step else sources[other].at[0, block % 2]

    def name(block):
        if not relative:
            return block
        return 2 * band_at(band_ref[0], 4 - block // 4, block // 2 % 2) + block % 2

    def send(block):
        slot = jnp.maximum(table_ref[name(block)], 0)
        return pltpu.make_async_copy(source(block), out_ref.at[slot], sems.at[block])

    for block in range(16):

        @pl.when(table_ref[name(block)] >= 0)
        def _():
            send(block).start()

    for block in range(16):

        @pl.when(table_ref[name(block)] >= 0)
        def _():
            send(block).wait()


def pack(table, band, *sources):
    shape, kind = sources[0].shape[2:], sources[0].dtype
    sources = [pltpu.with_memory_space_constraint(source, pltpu.VMEM) for source in sources]
    return pl.pallas_call(
        functools.partial(pack_kernel, len(sources) > 1),
        grid_spec=pltpu.PrefetchScalarGridSpec(
            num_scalar_prefetch=2,
            grid=(1,),
            in_specs=[pl.BlockSpec(memory_space=pltpu.VMEM)] * len(sources),
            out_specs=pl.BlockSpec(memory_space=pl.ANY),
            scratch_shapes=[pltpu.SemaphoreType.DMA((16,))],
        ),
        out_shape=jax.ShapeDtypeStruct((32,) + shape, kind),
        compiler_params=pltpu.CompilerParams(vmem_limit_bytes=VMEM_LIMIT),
        name="pack",
    )(table, band, *sources)


def image_kernel(chunks, ids_ref, offsets_ref, *refs):
    arrived = refs[:chunks]
    angle_ref, range_ref, out_ref, total, turned, angle = refs[chunks:]
    step = pl.program_id(0)
    heights = [part.shape[2] for part in arrived]

    @pl.when(step == 0)
    def _():
        angle[...] = jnp.transpose(angle_ref[...].astype(jnp.float32)).astype(jnp.bfloat16)

    @pl.when(step < 4)
    def _():
        total[...] = jnp.zeros_like(total)
        for slot in range(32):
            target = ids_ref[slot]

            @pl.when(target >= 0)
            def _():
                for chunk in range(chunks):
                    rows = pl.ds(sum(heights[:chunk]), heights[chunk])
                    total[target, :, rows, :] += arrived[chunk][slot].astype(jnp.float32)

        for image in range(8):
            both = [total[2 * image : 2 * image + 2, b].reshape(256, 128) for b in range(2)]
            both = jnp.concatenate(both, 1).astype(jnp.bfloat16)
            product = jnp.dot(angle[...], both, preferred_element_type=jnp.float32).astype(jnp.bfloat16)
            for b in range(2):
                rows = pl.ds(256 * image, 256)
                turned[2 * step + b, rows, :] = product[:, 128 * b : 128 * b + 128]

    @pl.when(step >= 4)
    def _():
        for one in range(2):
            start = offsets_ref[jnp.maximum(step - 4, 0) * 2 + one]
            columns = pl.ds(128 * one, 128)
            for half in range(2):
                rows = pl.ds(1024 * half, 1024)
                slab = jnp.concatenate([turned[start + i, rows, :] for i in range(3)], 1)
                product = jnp.dot(slab, range_ref[one], preferred_element_type=jnp.float32)
                out_ref[rows, columns] = product.astype(jnp.bfloat16)


def form_images(ids, offsets, arrived, angle, range_weights):
    chunks = len(arrived)
    return pl.pallas_call(
        functools.partial(image_kernel, chunks),
        grid_spec=pltpu.PrefetchScalarGridSpec(
            num_scalar_prefetch=2,
            grid=(8,),
            in_specs=[
                pl.BlockSpec((32, 2, part.shape[2], 128), lambda s, *_: (0, jnp.minimum(s, 3), 0, 0))
                for part in arrived
            ]
            + [
                pl.BlockSpec((256, 256), lambda s, *_: (0, 0)),
                pl.BlockSpec((2, 384, 128), lambda s, *_: (jnp.maximum(s - 4, 0), 0, 0)),
            ],
            out_specs=pl.BlockSpec((2048, 256), lambda s, *_: (0, jnp.maximum(s - 4, 0))),
            scratch_shapes=[
                pltpu.VMEM((16, 2, 128, 128), jnp.float32),
                pltpu.VMEM((8, 2048, 128), jnp.bfloat16),
                pltpu.VMEM((256, 256), jnp.bfloat16),
            ],
        ),
        out_shape=jax.ShapeDtypeStruct((2048, 1024), jnp.bfloat16),
        compiler_params=pltpu.CompilerParams(vmem_limit_bytes=VMEM_LIMIT),
        name="form_images",
    )(ids, offsets, *arrived, angle, range_weights)


def angle_matrix(steering, angle_weights):
    both = jnp.einsum("pya,sae->pyse", angle_weights, steering, preferred_element_type=jnp.float32)
    real, imag = both[:, :, 0], both[:, :, 1]
    full = jnp.stack([jnp.stack([real, -imag], 2), jnp.stack([imag, real], 2)], 0)
    full = full.astype(jnp.bfloat16).reshape(2, 2, 128, 2, 8, 8)
    return full.transpose(1, 5, 3, 4, 0, 2).reshape(256, 256)


def routing(merge_owner, merge_slot, ping_index):
    owners = merge_owner.reshape(16, 16)
    slots = merge_slot.reshape(16, 16)
    place = jnp.arange(16, dtype=jnp.int32)
    same = (owners[:, :, None] == owners[:, None, :]) & (place[None, :, None] > place[None, None, :])
    rank = jnp.sum(same.astype(jnp.int32), 2)
    leaving = jnp.where(owners >= 0, owners * 2 + rank, -1)
    table = lax.dynamic_index_in_dim(leaving, ping_index, 0, keepdims=False)
    pair = jnp.arange(2, dtype=jnp.int32)
    coming = (owners[:, None, :] == ping_index) & (rank[:, None, :] == pair[None, :, None])
    target = slots * 2 + place[None, :] % 2
    ids = jnp.sum(jnp.where(coming, target[:, None, :] + 1, 0), 2) - 1
    return table, ids.reshape(32)


def to_owners(some, table, band, source):
    def exchange(table, band, source):
        return lax.all_to_all(pack(table, band, source), "ping", split_axis=0, concat_axis=0, tiled=True)

    def nothing(table, band, source):
        return jnp.zeros((32,) + source.shape[2:], source.dtype)

    return lax.cond(some, exchange, nothing, table, band, source)


def flat(part):
    return part.reshape(part.shape[:3] + (-1, 128))


def ring_step(step, other):
    return [(band, ((band // 2 + step) % 4) * 2 + (band + other) % 2) for band in range(8)]


def on_device(echoes, replica, steering, angle_weights, range_weights, range_offsets, merge_owner, merge_slot):
    ping_index = lax.axis_index("ping")
    x = echoes.reshape(16, 8, 2, 64, 128).transpose(0, 1, 3, 2, 4).reshape(16, 8, 128, 128)
    table, ids = routing(merge_owner, merge_slot, ping_index)
    angle = angle_matrix(steering, angle_weights)
    band_index = lax.axis_index("band")
    band = band_index.reshape(1).astype(jnp.int32)
    (sent,) = compress(band, x, replica, 0, SPLIT, False)
    band_tile = lax.all_to_all(sent, "band", split_axis=0, concat_axis=0, tiled=True)
    same, other = compress(band, x, replica, SPLIT, 8 - SPLIT, True)
    other = lax.ppermute(other, "band", ring_step(0, 1))
    ring = [jnp.stack([same[step], other[step]]) for step in (1, 2, 3)]
    same, other = same[:1], other[:1]
    some = jnp.any(merge_owner >= 0)
    band_tile, table, ids, angle, some, same, other, *ring = lax.optimization_barrier(
        (band_tile, table, ids, angle, some, same, other, *ring)
    )
    ring = [lax.ppermute(part, "band", ring_step(step + 1, 0)) for step, part in enumerate(ring)]
    first = to_owners(some, table, band, flat(band_tile))
    first, *ring = lax.optimization_barrier((first, *ring))
    outgoing = pack(table, band, *[flat(part) for part in (same, other, *ring)])
    second = lax.all_to_all(outgoing, "ping", split_axis=0, concat_axis=0, tiled=True)
    arrived = [first, second]
    merged = form_images(ids, range_offsets, arrived, angle, range_weights)
    return merged.reshape(8, 2, 128, 1024)


def solution(mesh):
    placed = (
        P(("ping", "band"), None, None, None),
        P(),
        P(),
        P(),
        P("band", None, None),
        P("band"),
        P(),
        P(),
    )
    return jax.shard_map(
        on_device,
        mesh=mesh,
        in_specs=placed,
        out_specs=P("ping", None, None, "band"),
        check_vma=False,
    )
```

```python
import functools

import jax
import jax.numpy as jnp
from jax import lax
from jax.experimental import pallas as pl
from jax.experimental.pallas import tpu as pltpu
from jax.sharding import PartitionSpec as P

SPLIT = 3
VMEM_LIMIT = 56 * 1024 * 1024


def compress_kernel(relative, band_ref, x_ref, taps_ref, *refs):
    row = lax.broadcasted_iota(jnp.int32, (128, 128), 0)
    col = lax.broadcasted_iota(jnp.int32, (128, 128), 1)
    lower, upper = [], []
    for part in range(2):
        line = jnp.broadcast_to(taps_ref[0, part : part + 1, :].astype(jnp.float32), (128, 128))
        circulant = jnp.transpose(pltpu.roll(line, 0, 1, stride=1, stride_axis=0))
        lower.append(jnp.where(row >= col, circulant, 0.0))
        upper.append(jnp.where(row < col, circulant, 0.0))
    weights = jnp.concatenate(
        [
            jnp.concatenate([lower[0], -lower[1]], 1),
            jnp.concatenate([lower[1], lower[0]], 1),
            jnp.concatenate([upper[0], -upper[1]], 1),
            jnp.concatenate([upper[1], upper[0]], 1),
        ],
        0,
    ).astype(jnp.bfloat16)
    wanted = (row & 7) * 16 + ((row >> 3) & 7) * 2 + (row >> 6)
    permute = (wanted == col).astype(jnp.float32).astype(jnp.bfloat16)
    for block in range(2):
        real, imag = [], []
        for tile in range(8):
            rows = x_ref[8 * block : 8 * block + 8, 0, 16 * tile : 16 * tile + 16, :]
            moved = jnp.dot(permute, rows.reshape(128, 128), preferred_element_type=jnp.float32)
            real.append(moved[:64])
            imag.append(moved[64:])
        real = jnp.concatenate(real, 0)
        imag = jnp.concatenate(imag, 0)
        nothing = jnp.zeros((8, 128), jnp.float32)
        real_next = jnp.concatenate([real[8:], nothing], 0)
        imag_next = jnp.concatenate([imag[8:], nothing], 0)
        stacked = jnp.concatenate([real, imag, real_next, imag_next], 1).astype(jnp.bfloat16)
        product = jnp.dot(stacked, weights, preferred_element_type=jnp.float32)
        product = product.reshape(64, 8, 256)
        product = jnp.concatenate([product[:, :, :128], product[:, :, 128:]], 1)
        product = product.astype(jnp.bfloat16).reshape(8, 8, 16, 128)
        if not relative:
            refs[0][:, block, :, 0] = product
            continue
        held = refs[2]
        held[...] = product
        for step in range(4):
            for other in range(2):
                refs[other][step, block, :, 0] = held[band_at(band_ref[0], step, other)]


def band_at(band, step, other):
    return ((band >> 1) + step) % 4 * 2 + ((band & 1) + other) % 2


def compress(band, x, taps, first, count, relative):
    lead, outs = (4, 2) if relative else (8, 1)
    return pl.pallas_call(
        functools.partial(compress_kernel, relative),
        grid_spec=pltpu.PrefetchScalarGridSpec(
            num_scalar_prefetch=1,
            grid=(count,),
            in_specs=[
                pl.BlockSpec((16, 1, 128, 128), lambda i, *_: (0, first + i, 0, 0)),
                pl.BlockSpec((1, 2, 128), lambda i, *_: (first + i, 0, 0)),
            ],
            out_specs=[pl.BlockSpec((lead, 2, 8, 1, 16, 128), lambda i, *_: (0, 0, 0, i, 0, 0))] * outs,
            scratch_shapes=[pltpu.VMEM((8, 8, 16, 128), jnp.bfloat16)] * relative,
        ),
        out_shape=[jax.ShapeDtypeStruct((lead, 2, 8, count, 16, 128), jnp.bfloat16)] * outs,
        compiler_params=pltpu.CompilerParams(vmem_limit_bytes=VMEM_LIMIT),
        name="compress_relative" if relative else "compress",
    )(band, x, taps)


def pack_kernel(relative, table_ref, band_ref, *refs):
    sources, (out_ref, sems) = refs[:-2], refs[-2:]

    def source(block):
        if not relative:
            return sources[0].at[block // 2, block % 2]
        step, other = block // 4, block // 2 % 2
        return sources[step + 1].at[other, block % 2] if step else sources[other].at[0, block % 2]

    def name(block):
        if not relative:
            return block
        return 2 * band_at(band_ref[0], 4 - block // 4, block // 2 % 2) + block % 2

    def send(block):
        slot = jnp.maximum(table_ref[name(block)], 0)
        return pltpu.make_async_copy(source(block), out_ref.at[slot], sems.at[block])

    for block in range(16):

        @pl.when(table_ref[name(block)] >= 0)
        def _():
            send(block).start()

    for block in range(16):

        @pl.when(table_ref[name(block)] >= 0)
        def _():
            send(block).wait()


def pack(table, band, *sources):
    shape, kind = sources[0].shape[2:], sources[0].dtype
    sources = [pltpu.with_memory_space_constraint(source, pltpu.VMEM) for source in sources]
    return pl.pallas_call(
        functools.partial(pack_kernel, len(sources) > 1),
        grid_spec=pltpu.PrefetchScalarGridSpec(
            num_scalar_prefetch=2,
            grid=(1,),
            in_specs=[pl.BlockSpec(memory_space=pltpu.VMEM)] * len(sources),
            out_specs=pl.BlockSpec(memory_space=pl.ANY),
            scratch_shapes=[pltpu.SemaphoreType.DMA((16,))],
        ),
        out_shape=jax.ShapeDtypeStruct((32,) + shape, kind),
        compiler_params=pltpu.CompilerParams(vmem_limit_bytes=VMEM_LIMIT),
        name="pack",
    )(table, band, *sources)


def image_kernel(chunks, ids_ref, offsets_ref, *refs):
    arrived = refs[:chunks]
    angle_ref, range_ref, out_ref, total, turned, angle = refs[chunks:]
    step = pl.program_id(0)
    heights = [part.shape[2] for part in arrived]

    @pl.when(step == 0)
    def _():
        angle[...] = jnp.transpose(angle_ref[...].astype(jnp.float32)).astype(jnp.bfloat16)

    @pl.when(step < 4)
    def _():
        total[...] = jnp.zeros_like(total)
        for slot in range(32):
            target = ids_ref[slot]

            @pl.when(target >= 0)
            def _():
                for chunk in range(chunks):
                    rows = pl.ds(sum(heights[:chunk]), heights[chunk])
                    total[target, :, rows, :] += arrived[chunk][slot].astype(jnp.float32)

        for image in range(8):
            both = [total[2 * image : 2 * image + 2, b].reshape(256, 128) for b in range(2)]
            both = jnp.concatenate(both, 1).astype(jnp.bfloat16)
            product = jnp.dot(angle[...], both, preferred_element_type=jnp.float32).astype(jnp.bfloat16)
            for b in range(2):
                rows = pl.ds(256 * image, 256)
                turned[2 * step + b, rows, :] = product[:, 128 * b : 128 * b + 128]

    @pl.when(step >= 4)
    def _():
        for one in range(2):
            start = offsets_ref[jnp.maximum(step - 4, 0) * 2 + one]
            columns = pl.ds(128 * one, 128)
            for half in range(2):
                rows = pl.ds(1024 * half, 1024)
                slab = jnp.concatenate([turned[start + i, rows, :] for i in range(3)], 1)
                product = jnp.dot(slab, range_ref[one], preferred_element_type=jnp.float32)
                out_ref[rows, columns] = product.astype(jnp.bfloat16)


def form_images(ids, offsets, arrived, angle, range_weights):
    chunks = len(arrived)
    return pl.pallas_call(
        functools.partial(image_kernel, chunks),
        grid_spec=pltpu.PrefetchScalarGridSpec(
            num_scalar_prefetch=2,
            grid=(8,),
            in_specs=[
                pl.BlockSpec((32, 2, part.shape[2], 128), lambda s, *_: (0, jnp.minimum(s, 3), 0, 0))
                for part in arrived
            ]
            + [
                pl.BlockSpec((256, 256), lambda s, *_: (0, 0)),
                pl.BlockSpec((2, 384, 128), lambda s, *_: (jnp.maximum(s - 4, 0), 0, 0)),
            ],
            out_specs=pl.BlockSpec((2048, 256), lambda s, *_: (0, jnp.maximum(s - 4, 0))),
            scratch_shapes=[
                pltpu.VMEM((16, 2, 128, 128), jnp.float32),
                pltpu.VMEM((8, 2048, 128), jnp.bfloat16),
                pltpu.VMEM((256, 256), jnp.bfloat16),
            ],
        ),
        out_shape=jax.ShapeDtypeStruct((2048, 1024), jnp.bfloat16),
        compiler_params=pltpu.CompilerParams(vmem_limit_bytes=VMEM_LIMIT),
        name="form_images",
    )(ids, offsets, *arrived, angle, range_weights)


def angle_matrix(steering, angle_weights):
    both = jnp.einsum("pya,sae->pyse", angle_weights, steering, preferred_element_type=jnp.float32)
    real, imag = both[:, :, 0], both[:, :, 1]
    full = jnp.stack([jnp.stack([real, -imag], 2), jnp.stack([imag, real], 2)], 0)
    full = full.astype(jnp.bfloat16).reshape(2, 2, 128, 2, 8, 8)
    return full.transpose(1, 5, 3, 4, 0, 2).reshape(256, 256)


def routing(merge_owner, merge_slot, ping_index):
    owners = merge_owner.reshape(16, 16)
    slots = merge_slot.reshape(16, 16)
    place = jnp.arange(16, dtype=jnp.int32)
    same = (owners[:, :, None] == owners[:, None, :]) & (place[None, :, None] > place[None, None, :])
    rank = jnp.sum(same.astype(jnp.int32), 2)
    leaving = jnp.where(owners >= 0, owners * 2 + rank, -1)
    table = lax.dynamic_index_in_dim(leaving, ping_index, 0, keepdims=False)
    pair = jnp.arange(2, dtype=jnp.int32)
    coming = (owners[:, None, :] == ping_index) & (rank[:, None, :] == pair[None, :, None])
    target = slots * 2 + place[None, :] % 2
    ids = jnp.sum(jnp.where(coming, target[:, None, :] + 1, 0), 2) - 1
    return table, ids.reshape(32)


def to_owners(some, table, band, source):
    def exchange(table, band, source):
        return lax.all_to_all(pack(table, band, source), "ping", split_axis=0, concat_axis=0, tiled=True)

    def nothing(table, band, source):
        return jnp.zeros((32,) + source.shape[2:], source.dtype)

    return lax.cond(some, exchange, nothing, table, band, source)


def flat(part):
    return part.reshape(part.shape[:3] + (-1, 128))


def ring_step(step, other):
    return [(band, ((band // 2 + step) % 4) * 2 + (band + other) % 2) for band in range(8)]


def on_device(echoes, replica, steering, angle_weights, range_weights, range_offsets, merge_owner, merge_slot):
    ping_index = lax.axis_index("ping")
    x = echoes.reshape(16, 8, 2, 64, 128).transpose(0, 1, 3, 2, 4).reshape(16, 8, 128, 128)
    table, ids = routing(merge_owner, merge_slot, ping_index)
    angle = angle_matrix(steering, angle_weights)
    band_index = lax.axis_index("band")
    band = band_index.reshape(1).astype(jnp.int32)
    (sent,) = compress(band, x, replica, 0, SPLIT, False)
    band_tile = lax.all_to_all(sent, "band", split_axis=0, concat_axis=0, tiled=True)
    same, other = compress(band, x, replica, SPLIT, 8 - SPLIT, True)
    other = lax.ppermute(other, "band", ring_step(0, 1))
    ring = [jnp.stack([same[step], other[step]]) for step in (1, 2, 3)]
    same, other = same[:1], other[:1]
    some = jnp.any(merge_owner >= 0)
    band_tile, table, ids, angle, some, same, other = lax.optimization_barrier(
        (band_tile, table, ids, angle, some, same, other)
    )
    ring = [lax.ppermute(part, "band", ring_step(step + 1, 0)) for step, part in enumerate(ring)]
    first = to_owners(some, table, band, flat(band_tile))
    first, *ring = lax.optimization_barrier((first, *ring))
    outgoing = pack(table, band, *[flat(part) for part in (same, other, *ring)])
    second = lax.all_to_all(outgoing, "ping", split_axis=0, concat_axis=0, tiled=True)
    arrived = [first, second]
    merged = form_images(ids, range_offsets, arrived, angle, range_weights)
    return merged.reshape(8, 2, 128, 1024)


def solution(mesh):
    placed = (
        P(("ping", "band"), None, None, None),
        P(),
        P(),
        P(),
        P("band", None, None),
        P("band"),
        P(),
        P(),
    )
    return jax.shard_map(
        on_device,
        mesh=mesh,
        in_specs=placed,
        out_specs=P("ping", None, None, "band"),
        check_vma=False,
    )
```
